1024 devices in a mesh: walk: 128 (over z, x, core), chol: 8 (over y).
Axes of the slice: x: 4, y: 8, z: 16, core: 2. Of those that a mesh axis runs over, the one named last changes fastest.
Arguments:
- walkers: bfloat16 [768, 2048, 128], P('walk', 'chol'), may hold values from -6 to 6
- inv_intersection: bfloat16 [768, 128, 128], P('walk'), may hold values from -0.5 to 0.5
- fields: bfloat16 [768, 16], P('walk', 'chol'), may hold values from -5 to 5
- cholesky: bfloat16 [16, 512, 2048], P('chol'), may hold values from -0.125 to 0.125
- trial_rows: bfloat16 [512, 128], replicated, may hold values from -0.234375 to 0.234375
- counts: int32 [128], replicated, may hold values from 1 to 6, as said below
- partner: int32 [128], replicated, may hold values from 0 to 127, as said below
Outputs:
- new_walkers: bfloat16 [512, 512, 128], P('walk', 'chol')
- log_weight: float32 [512], P('walk')
The draws below stay inside these ranges and needn't reach their ends.
Inputs may be any that keep to these rules, and one draw needn't show every extreme that they name: `counts`: of w and partner[w], exactly one holds more than 4 walkers, and the other holds at most 8 minus that count; some walk index holds exactly 6 walkers. partner[partner[w]] = w, and partner[w] differs from w in exactly one bit.
All inputs are finite; a program needn't handle non-finite values.
Results may differ from the reference program's by a relative error of at most 0.0075.
Values may be sent and summed in bfloat16 or wider, within the bound.
No kernel may reach another device: no remote copies, remote signals or barrier semaphores. Data moves between devices by JAX's collectives and lax.ppermute only.
A program may use at most 32 MiB of HBM per device.

```python
import jax
import jax.numpy as jnp
from jax import lax

NORB = 2048
NOCC = 128
NCHOL = 16
ROWS_DEV = 64
R = 512
LIVE = 4
MOVE = 2
SLOTS = 6
WALK_DEVS = 128
WALKERS = 768
BALANCED = 512
N_CHOL = 8


def pairing(key):
    base_key = jax.random.fold_in(key, 11)
    key_order, key_coin, key_move, key_count = jax.random.split(base_key, 4)
    key_label = jax.random.fold_in(base_key, 23)
    bit_count = WALK_DEVS.bit_length() - 1
    device_ids = jnp.arange(WALK_DEVS, dtype=jnp.int32)
    translate = jax.random.randint(key_label, (), 0, WALK_DEVS).astype(jnp.int32)
    labels = jnp.bitwise_xor(device_ids, translate)
    order = jax.random.permutation(key_order, bit_count).astype(jnp.int32)
    chosen_bit = jnp.zeros((WALK_DEVS,), jnp.int32) - 1
    taken_mask = jnp.int32(0)
    for level in range(bit_count):
        level_bit = order[level]
        group_ids = jnp.bitwise_and(labels, taken_mask)
        level_coin = jax.random.randint(jax.random.fold_in(base_key, 100 + level), (WALK_DEVS,), 0, 4)[group_ids]
        if level == bit_count - 1:
            settle = chosen_bit < 0
        elif level == 0:
            settle = (chosen_bit < 0) & (level_coin == 0)
        else:
            settle = (chosen_bit < 0) & (level_coin >= 2)
        chosen_bit = jnp.where(settle, level_bit, chosen_bit)
        taken_mask = jnp.bitwise_or(taken_mask, jnp.left_shift(jnp.int32(1), level_bit))
    partner = jnp.bitwise_xor(device_ids, jnp.left_shift(jnp.int32(1), chosen_bit))
    pair_low = jnp.minimum(device_ids, partner)
    pair_high = jnp.maximum(device_ids, partner)
    last_id = WALK_DEVS - 1
    first_pair = pair_low == 0
    last_pair = pair_high == last_id
    coin_flip = jax.random.randint(key_coin, (WALK_DEVS,), 0, 2)
    surplus = (coin_flip[pair_low] == 1) == (device_ids == pair_low)
    surplus = jnp.where(first_pair, device_ids != 0, jnp.where(last_pair, device_ids != last_id, surplus))
    moved_count = jax.random.randint(key_move, (WALK_DEVS,), 1, MOVE + 1)[pair_low]
    moved_count = jnp.where(first_pair | last_pair, MOVE, moved_count)
    deficit_count = jax.random.randint(key_count, (WALK_DEVS,), 0, 1 << 20) % (LIVE - moved_count) + 1
    counts = jnp.where(surplus, LIVE + moved_count, deficit_count)
    return (counts.astype(jnp.int32), partner.astype(jnp.int32))


def draw_counts(key, part):
    return pairing(key)[0]


def draw_partner(key, part):
    return pairing(key)[1]


def block_levels(own_key, dims, pieces, low, high):
    def one(position, blocks):
        steps = jax.random.uniform(jax.random.fold_in(jax.random.fold_in(own_key, 6), position), (blocks,), jnp.float32, low / len(pieces), high / len(pieces))
        return jnp.repeat(jnp.exp(steps), dims[position] // blocks).reshape((-1,) + (1,) * (len(dims) - position - 1))

    factor_of = one(*pieces[0])
    for cut in pieces[1:]:
        factor_of = factor_of * one(*cut)
    return factor_of


def gaussian(own_key, dims, width, most, cuts=(), kind=jnp.bfloat16):
    array = jax.random.normal(own_key, dims, jnp.float32) * width
    if len(cuts) > 0:
        array = block_levels(own_key, dims, cuts, -0.22, 0.18) * array
    return jnp.clip(array, min=-most, max=most).astype(kind)


def setup_inputs(seed: int = 0) -> dict:
    key_list = jax.random.split(jax.random.key(seed), 8)
    walkers = gaussian(key_list[0], (WALKERS, NORB, NOCC), 1.0, 6.0, ((0, 128), (1, 8)))
    inv_intersection = gaussian(key_list[1], (WALKERS, NOCC, NOCC), NOCC ** -0.5, 0.5, ((0, 128),))
    fields = gaussian(key_list[2], (WALKERS, NCHOL), 1.0, 5.0, ((0, 128), (1, 8)))
    cholesky = gaussian(key_list[3], (NCHOL, R, NORB), NORB ** -0.5, 0.125, ((0, 8),))
    trial_rows = gaussian(key_list[4], (R, NOCC), (10.0 / (R * NOCC) ** 0.5), 0.234375)
    counts = draw_counts(jax.random.fold_in(key_list[7], 71), 0)
    partner = draw_partner(jax.random.fold_in(key_list[7], 71), 0)
    return {"walkers": walkers, "inv_intersection": inv_intersection, "fields": fields, "cholesky": cholesky, "trial_rows": trial_rows, "counts": counts, "partner": partner}


STEP_ROOT = 0.1


def expand_mask(mask_in, target):
    return mask_in.reshape(mask_in.shape + (1,) * (target.ndim - mask_in.ndim))


def select_slots(own_part, arriving, own_mask, incoming):
    arrived = jnp.zeros_like(own_part)
    for slot_num in range(MOVE):
        flag = incoming[:, :, slot_num]
        arrived = jnp.where(expand_mask(flag, own_part), arriving[:, slot_num:slot_num + 1], arrived)
    return jnp.where(expand_mask(own_mask, own_part), own_part, arrived)


def reference(walkers, inv_intersection, fields, cholesky, trial_rows, counts, partner):
    grouped = walkers.reshape(WALK_DEVS, SLOTS, NORB, NOCC)
    grouped_minv = inv_intersection.reshape(WALK_DEVS, SLOTS, NOCC, NOCC)
    grouped_fields = fields.reshape(WALK_DEVS, SLOTS, NCHOL)
    mate_count = counts[partner]
    arriving_count = jnp.maximum(mate_count - LIVE, 0)
    slot_ids = jnp.arange(LIVE, dtype=jnp.int32)
    own_mask = slot_ids[None, :] < jnp.minimum(counts, LIVE)[:, None]
    move_ids = jnp.arange(MOVE, dtype=jnp.int32)
    incoming = (slot_ids[None, :, None] - counts[:, None, None] == move_ids[None, None, :]) & (move_ids[None, None, :] < arriving_count[:, None, None])
    live = own_mask | jnp.any(incoming, axis=2)
    phi = select_slots(grouped[:, :LIVE], grouped[partner, LIVE:], own_mask, incoming)
    minv = select_slots(grouped_minv[:, :LIVE], grouped_minv[partner, LIVE:], own_mask, incoming)
    field_vals = select_slots(grouped_fields[:, :LIVE], grouped_fields[partner, LIVE:], own_mask, incoming)
    chol_wide = cholesky.astype(jnp.float32)
    trial_wide = trial_rows.astype(jnp.float32)

    def one_group(inputs):
        phi_group, minv_group, field_group, live_group = inputs
        products = jnp.einsum('grk,wkn->wgrn', chol_wide, phi_group.astype(jnp.float32))
        weighted = jnp.einsum('rb,wab->wra', trial_wide, minv_group.astype(jnp.float32))
        force_bias = -STEP_ROOT * jnp.einsum('wgrn,wrn->wg', products, weighted)
        field_wide = field_group.astype(jnp.float32)
        shifted = STEP_ROOT * (field_wide - force_bias)
        increment = jnp.einsum('wg,wgrn->wrn', shifted, products)
        log_terms = jnp.sum(field_wide * force_bias - 0.5 * force_bias * force_bias, axis=1)
        window = phi_group.reshape(LIVE, N_CHOL, NORB // N_CHOL, NOCC)[:, :, :ROWS_DEV].reshape(LIVE, R, NOCC)
        live_wide = live_group.astype(jnp.float32)
        new_rows = (live_wide[:, None, None] * (window.astype(jnp.float32) + increment)).astype(jnp.bfloat16)
        return new_rows, live_wide * log_terms

    new_rows, log_terms = lax.map(one_group, (phi, minv, field_vals, live))
    return new_rows.reshape(BALANCED, R, NOCC), log_terms.reshape(BALANCED)
```

```python
import jax
import jax.numpy as jnp
from jax import lax
from jax.experimental import pallas as pl
from jax.experimental.pallas import tpu as pltpu
from jax.sharding import PartitionSpec as P

ROWS_DEV = 64
LIVE = 4
MOVE = 2
STEP_ROOT = 0.1
N_CHOL = 8
OFFSETS = (0, -1, 1, -2, 2, -3, 3, -4)
TILE = 16


def ring(block):
    up = [(i, (i + 1) % N_CHOL) for i in range(N_CHOL)]
    down = [(i, (i - 1) % N_CHOL) for i in range(N_CHOL)]
    parts, low, high = [block], block, block
    for step in range(N_CHOL // 2):
        low = lax.ppermute(low, "chol", up)
        parts.append(low)
        if step < N_CHOL // 2 - 1:
            high = lax.ppermute(high, "chol", down)
            parts.append(high)
    return parts


def pair_kernel(late, blocks, x, *refs):
    parts, rest = refs[:N_CHOL], refs[N_CHOL:]
    if late:
        chol, trial, before, out, buf, acc, minv, sems = rest
    else:
        chol, trial, minv_in, out, buf, acc, sems = rest
    step = pl.program_id(0)
    stride = buf.shape[1] // 2
    rows = stride - TILE if late else stride

    def copy(d):
        return pltpu.make_async_copy(parts[d], buf.at[d], sems.at[d])

    @pl.when(step == 0)
    def _():
        for d in range(N_CHOL):
            copy(d).start()
        acc[...] = jnp.zeros_like(acc)

    pltpu.make_async_copy(parts[0], buf.at[step], sems.at[step]).wait()
    phi = jnp.concatenate([buf[step, :rows], buf[step, stride : stride + rows]], axis=1)
    for g in range(2):
        acc[g] += jnp.dot(chol[g], phi, preferred_element_type=jnp.float32)

    @pl.when(step == N_CHOL - 1)
    def _():
        base = LIVE // 2 if late else 0
        lanes = out.shape[2]
        row_id = lax.broadcasted_iota(jnp.int32, (TILE, lanes), 0)
        lane_id = lax.broadcasted_iota(jnp.int32, (TILE, lanes), 1)
        logs = jnp.zeros((TILE, lanes), jnp.float32)
        if late:
            logs = before[0, 2 * ROWS_DEV :].astype(jnp.float32)
            for d in range(N_CHOL):
                spot = pl.ds(pl.multiple_of(blocks[d] * TILE, TILE), TILE)
                for q in range(2):
                    minv[q, spot] = buf[d, q * stride + rows : (q + 1) * stride]
        for q in range(2):
            inv = minv[q] if late else minv_in[q]
            weighted = lax.dot_general(
                trial[...], inv, (((1,), (1,)), ((), ())), preferred_element_type=jnp.float32
            )
            total = jnp.zeros_like(weighted)
            log = jnp.zeros((1, 1), jnp.float32)
            for g in range(2):
                product = acc[g, :, q * lanes : (q + 1) * lanes]
                bias = -STEP_ROOT * jnp.sum(product * weighted, keepdims=True)
                field = x[base + q, g]
                total += STEP_ROOT * (field - bias) * product
                log += field * bias - 0.5 * bias * bias
            spread = total.astype(jnp.bfloat16).reshape(N_CHOL, ROWS_DEV, lanes)
            first = (base + q) * ROWS_DEV
            out[:, first : first + ROWS_DEV] = spread
            high = log.astype(jnp.bfloat16).astype(jnp.float32)
            here = row_id == base + q
            logs = jnp.where(here & (lane_id == 0), high, logs)
            logs = jnp.where(here & (lane_id == 1), log - high, logs)
        if late:
            out[:, : 2 * ROWS_DEV] = before[:, : 2 * ROWS_DEV]
        end = (base + 2) * ROWS_DEV
        for k in range(N_CHOL):
            out[k, end : end + TILE] = logs.astype(jnp.bfloat16)


def pair_call(late, blocks, x, parts, cholesky, trial, extra):
    rows, lanes = parts[0].shape
    vectors, window, orbitals = cholesky.shape
    depth = orbitals // N_CHOL
    out_rows = (LIVE if late else LIVE // 2) * ROWS_DEV + TILE
    whole = pl.BlockSpec(memory_space=pltpu.VMEM)
    scratch = [
        pltpu.VMEM((N_CHOL, rows, lanes), jnp.bfloat16),
        pltpu.VMEM((vectors, window, 2 * lanes), jnp.float32),
    ]
    if late:
        scratch.append(pltpu.VMEM((2, lanes, lanes), jnp.bfloat16))
    scratch.append(pltpu.SemaphoreType.DMA((N_CHOL,)))

    def body(*refs):
        pair_kernel(late, *refs)

    grid_spec = pltpu.PrefetchScalarGridSpec(
        num_scalar_prefetch=2,
        grid=(N_CHOL,),
        in_specs=[pl.BlockSpec(memory_space=pl.ANY)] * N_CHOL
        + [pl.BlockSpec((vectors, window, depth), lambda d, blocks, x: (0, 0, blocks[d]))]
        + [whole, whole],
        out_specs=whole,
        scratch_shapes=scratch,
    )
    flops = 4 * vectors * window * orbitals * lanes
    return pl.pallas_call(
        body,
        grid_spec=grid_spec,
        out_shape=jax.ShapeDtypeStruct((N_CHOL, out_rows, lanes), jnp.bfloat16),
        name="late_pair" if late else "early_pair",
        cost_estimate=pl.CostEstimate(flops=flops, bytes_accessed=6 << 20, transcendentals=0),
    )(blocks, x, *parts, cholesky, trial, extra)


def finish_kernel(order, got, window, out, log_out):
    for s in range(LIVE):
        spot = order[s]
        live = order[LIVE + s] > 0
        rows = pl.ds(pl.multiple_of(spot * ROWS_DEV, ROWS_DEV), ROWS_DEV)
        total = window[rows].astype(jnp.float32)
        for k in range(N_CHOL):
            total += got[k, rows].astype(jnp.float32)
        out[s] = jnp.where(live, total, 0.0).astype(jnp.bfloat16)
        tile = jnp.zeros((TILE, got.shape[2]), jnp.float32)
        for k in range(N_CHOL):
            tile += got[k, LIVE * ROWS_DEV :].astype(jnp.float32)
        row_id = lax.broadcasted_iota(jnp.int32, tile.shape, 0)
        log = jnp.sum(jnp.where(row_id == spot, tile, 0.0))
        log_out[s] = jnp.where(live, log, 0.0)


def finish_call(order, got, window):
    lanes = got.shape[2]
    whole = pl.BlockSpec(memory_space=pltpu.VMEM)
    scalars = pl.BlockSpec(memory_space=pltpu.SMEM)
    return pl.pallas_call(
        finish_kernel,
        in_specs=[scalars, whole, whole],
        out_specs=(whole, scalars),
        out_shape=(
            jax.ShapeDtypeStruct((LIVE, ROWS_DEV, lanes), jnp.bfloat16),
            jax.ShapeDtypeStruct((LIVE,), jnp.float32),
        ),
        name="finish",
    )(order, got, window)


def shards(walkers, inv_intersection, fields, cholesky, trial_rows, counts, partner):
    walk_index = lax.axis_index("walk")
    chol_index = lax.axis_index("chol")
    own_count = counts[walk_index]
    mate_id = partner[walk_index]
    arriving_count = jnp.maximum(counts[mate_id] - LIVE, 0)
    distance = jnp.bitwise_xor(mate_id, walk_index)
    walk_size = lax.axis_size("walk")
    rows = walkers.shape[1]
    lanes = walkers.shape[2]

    inv_rows = lax.dynamic_slice_in_dim(inv_intersection, chol_index * TILE, TILE, 1)
    packed = jnp.concatenate([walkers[2:], inv_rows[2:]], axis=1)
    field_rows = jnp.pad(fields[LIVE:], ((0, TILE - MOVE), (0, lanes - fields.shape[1])))
    stride = rows + TILE
    outgoing = jnp.concatenate([packed[2:].reshape(MOVE * stride, lanes), field_rows], axis=0)

    received = jnp.zeros_like(outgoing)
    for bit in reversed(range(walk_size.bit_length() - 1)):
        route = [(i, i ^ 1 << bit) for i in range(walk_size)]
        fetched = lax.ppermute(outgoing, "walk", route)
        received = jnp.where(distance == 1 << bit, fetched, received)

    early = walkers[:2].reshape(2 * rows, lanes)
    early_parts = ring(early)

    keep = own_count > jnp.array([2, 3], jnp.int32)
    moved = received[: MOVE * stride].reshape(MOVE, stride, lanes)[::-1]
    late = jnp.where(keep[:, None, None], packed[:2], moved)
    moved_fields = received[MOVE * stride : MOVE * stride + MOVE, : fields.shape[1]][::-1]
    late_fields = jnp.where(keep[:, None], fields[2:LIVE], moved_fields)
    x = jnp.concatenate([fields[:2], late_fields], axis=0).astype(jnp.float32)
    late_parts = ring(late.reshape(2 * stride, lanes))

    blocks = (chol_index + jnp.array(OFFSETS, jnp.int32)) & (N_CHOL - 1)
    first = pair_call(False, blocks, x, early_parts, cholesky, trial_rows, inv_intersection[:2])
    sums = pair_call(True, blocks, x, late_parts, cholesky, trial_rows, first)
    sums = lax.all_to_all(sums, "chol", 0, 0, tiled=True)

    slots = jnp.arange(LIVE, dtype=jnp.int32)
    own = slots < own_count
    moved_slot = slots - own_count
    live = own | (moved_slot < arriving_count)
    spot = jnp.where(own, slots, jnp.clip(LIVE - 1 - moved_slot, 0, LIVE - 1))
    order = jnp.concatenate([spot, live.astype(jnp.int32)])
    window = jnp.concatenate([walkers[:2, :ROWS_DEV], late[:, :ROWS_DEV]], axis=0)
    return tuple(finish_call(order, sums, window.reshape(LIVE * ROWS_DEV, lanes)))


def solution(mesh):
    in_specs = (
        P("walk", "chol", None),
        P("walk", None, None),
        P("walk", "chol"),
        P("chol", None, None),
        P(),
        P(),
        P(),
    )
    out_specs = (P("walk", "chol", None), P("walk"))
    return jax.shard_map(shards, mesh=mesh, in_specs=in_specs, out_specs=out_specs, check_vma=False)
```

```python
import jax
import jax.numpy as jnp
from jax import lax
from jax.experimental import pallas as pl
from jax.experimental.pallas import tpu as pltpu
from jax.sharding import PartitionSpec as P

ROWS_DEV = 64
LIVE = 4
MOVE = 2
STEP_ROOT = 0.1
N_CHOL = 8
OFFSETS = (0, -1, 1, -2, 2, -3, 3, -4)
TILE = 16
ORBS = 256
STRIDE = ORBS + TILE
STARTS = (0, ORBS, 2 * ORBS, 2 * ORBS + STRIDE)
RING_ROWS = 2 * ORBS + 2 * STRIDE
FIELD_ROW = MOVE * STRIDE

ANY = pl.BlockSpec(memory_space=pl.ANY)
WHOLE = pl.BlockSpec(memory_space=pltpu.VMEM)
SCALARS = pl.BlockSpec(memory_space=pltpu.SMEM)
F32 = jnp.float32
BF16 = jnp.bfloat16


def ring(block):
    up = [(i, (i + 1) % N_CHOL) for i in range(N_CHOL)]
    down = [(i, (i - 1) % N_CHOL) for i in range(N_CHOL)]
    parts, low, high = [block], block, block
    for step in range(N_CHOL // 2):
        low = lax.ppermute(low, "chol", up)
        parts.append(low)
        if step < N_CHOL // 2 - 1:
            high = lax.ppermute(high, "chol", down)
            parts.append(high)
    return parts


def inv_rows(inv, slot):
    share = pl.multiple_of(lax.axis_index("chol") * TILE, TILE)
    return inv.at[slot, pl.ds(share, TILE)]


def pack_kernel(walkers, inv, fields, out, sems):
    copies = []
    for j in range(MOVE):
        rows = out.at[pl.ds(j * STRIDE, ORBS)]
        copies.append(pltpu.make_async_copy(walkers.at[LIVE + j], rows, sems.at[2 * j]))
        rows = out.at[pl.ds(j * STRIDE + ORBS, TILE)]
        copies.append(pltpu.make_async_copy(inv_rows(inv, LIVE + j), rows, sems.at[2 * j + 1]))
    for copy in copies:
        copy.start()
    out[FIELD_ROW:] = jnp.zeros((TILE, out.shape[1]), BF16)
    out[FIELD_ROW : FIELD_ROW + fields.shape[0], : fields.shape[1]] = fields[...]
    for copy in copies:
        copy.wait()


def pack_call(walkers, inv, fields):
    return pl.pallas_call(
        pack_kernel,
        in_specs=[ANY, ANY, WHOLE],
        out_specs=WHOLE,
        out_shape=jax.ShapeDtypeStruct((FIELD_ROW + TILE, walkers.shape[2]), BF16),
        scratch_shapes=[pltpu.SemaphoreType.DMA((2 * MOVE,))],
        name="pack",
    )(walkers, inv, fields)


def merge_kernel(bits, counts, partner, fields, walkers, inv, *refs):
    received, (out, x, moved, sems) = refs[:bits], refs[bits:]
    walk = lax.axis_index("walk")
    own = counts[walk]
    distance = jnp.bitwise_xor(partner[walk], walk)

    def start(slot, source, size, sem, first=0):
        rows = out.at[pl.ds(STARTS[slot] + first, size)]
        pltpu.make_async_copy(source, rows, sems.at[sem]).start()

    start(0, walkers.at[0], ORBS, 0)
    start(1, walkers.at[1], ORBS, 1)
    for slot in (2, 3):

        @pl.when(own > slot)
        def _():
            start(slot, walkers.at[slot], ORBS, slot)
            start(slot, inv_rows(inv, slot), TILE, slot + 2, ORBS)

    for bit in range(bits):

        @pl.when(distance == 1 << bit)
        def _():
            block = received[bit]
            pltpu.make_async_copy(block.at[pl.ds(FIELD_ROW, TILE)], moved, sems.at[6]).start()
            for slot in (2, 3):

                @pl.when(own <= slot)
                def _():
                    first = (3 - slot) * STRIDE
                    start(slot, block.at[pl.ds(first, ORBS)], ORBS, slot)
                    start(slot, block.at[pl.ds(first + ORBS, TILE)], TILE, slot + 2, ORBS)

    def wait(slot, size, sem, first=0):
        rows = out.at[pl.ds(STARTS[slot] + first, size)]
        pltpu.make_async_copy(rows, rows, sems.at[sem]).wait()

    pltpu.make_async_copy(moved, moved, sems.at[6]).wait()
    mine = fields[...].astype(F32)
    theirs = moved[: fields.shape[0], : fields.shape[1]].astype(F32)
    x[...] = jnp.zeros_like(x)
    for slot in range(LIVE):
        row = mine[slot : slot + 1]
        if slot > 1:
            sent = LIVE + 3 - slot
            row = jnp.where(own > slot, row, theirs[sent : sent + 1])
        x[slot : slot + 1, : fields.shape[1]] = row
    for slot in range(LIVE):
        wait(slot, ORBS, slot)
        if slot > 1:
            wait(slot, TILE, slot + 2, ORBS)


def merge_call(counts, partner, fields, walkers, inv, received):
    bits, lanes = len(received), walkers.shape[2]

    def body(*refs):
        merge_kernel(bits, *refs)

    return pl.pallas_call(
        body,
        in_specs=[SCALARS, SCALARS, WHOLE, ANY, ANY] + [ANY] * bits,
        out_specs=(WHOLE, WHOLE),
        out_shape=(
            jax.ShapeDtypeStruct((RING_ROWS, lanes), BF16),
            jax.ShapeDtypeStruct((8, lanes), F32),
        ),
        scratch_shapes=[pltpu.VMEM((TILE, lanes), BF16), pltpu.SemaphoreType.DMA((7,))],
        name="merge",
    )(counts, partner, fields, walkers, inv, *received)


def product_kernel(x, chol, trial, inv, *refs):
    parts, (out, minv) = refs[:N_CHOL], refs[N_CHOL:]
    lanes = out.shape[2]
    me = lax.axis_index("chol")
    owners = [jnp.bitwise_and(me + offset, N_CHOL - 1) for offset in OFFSETS]
    columns = [pl.ds(pl.multiple_of(owner * ORBS, ORBS), ORBS) for owner in owners]
    for owner, part in zip(owners, parts):
        share = pl.ds(pl.multiple_of(owner * TILE, TILE), TILE)
        for q in range(2):
            first = STARTS[2 + q] + ORBS
            minv[q, share] = part[first : first + TILE]
    row_id = lax.broadcasted_iota(jnp.int32, (TILE, lanes), 0)
    lane_id = lax.broadcasted_iota(jnp.int32, (TILE, lanes), 1)
    logs = jnp.zeros((TILE, lanes), F32)
    for pair in range(2):
        slots = (2 * pair, 2 * pair + 1)
        phi = jnp.concatenate(
            [
                jnp.concatenate([part[STARTS[s] : STARTS[s] + ORBS] for s in slots], axis=1)
                for part in parts
            ],
            axis=0,
        )
        products = []
        for g in range(chol.shape[0]):
            rows = jnp.concatenate([chol[g, :, spot] for spot in columns], axis=1)
            products.append(jnp.dot(rows, phi, preferred_element_type=F32))
        for q, slot in enumerate(slots):
            weighted = lax.dot_general(
                trial[...],
                minv[q] if pair else inv[q],
                (((1,), (1,)), ((), ())),
                preferred_element_type=F32,
            )
            total = jnp.zeros_like(weighted)
            log = jnp.zeros((1, 1), F32)
            for g, both in enumerate(products):
                product = both[:, q * lanes : (q + 1) * lanes]
                bias = -STEP_ROOT * jnp.sum(product * weighted, keepdims=True)
                field = x[slot : slot + 1, g : g + 1]
                total += STEP_ROOT * (field - bias) * product
                log += field * bias - 0.5 * bias * bias
            spread = total.astype(BF16).reshape(N_CHOL, ROWS_DEV, lanes)
            out[:, slot * ROWS_DEV : (slot + 1) * ROWS_DEV] = spread
            high = log.astype(BF16).astype(F32)
            here = row_id == slot
            logs = jnp.where(here & (lane_id == 0), high, logs)
            logs = jnp.where(here & (lane_id == 1), log - high, logs)
    for k in range(N_CHOL):
        out[k, LIVE * ROWS_DEV :] = logs.astype(BF16)


def product_call(x, cholesky, trial, inv, parts):
    lanes = trial.shape[1]
    vectors, window, orbitals = cholesky.shape
    flops = 2 * LIVE * vectors * window * orbitals * lanes
    return pl.pallas_call(
        product_kernel,
        in_specs=[WHOLE] * (4 + N_CHOL),
        out_specs=WHOLE,
        out_shape=jax.ShapeDtypeStruct((N_CHOL, LIVE * ROWS_DEV + TILE, lanes), BF16),
        scratch_shapes=[pltpu.VMEM((2, lanes, lanes), BF16)],
        name="products",
        cost_estimate=pl.CostEstimate(flops=flops, bytes_accessed=6 << 20, transcendentals=0),
    )(x, cholesky, trial, inv, *parts)


def finish_kernel(counts, partner, got, block, out, log_out):
    walk = lax.axis_index("walk")
    own = jnp.minimum(counts[walk], LIVE)
    arriving = jnp.maximum(counts[partner[walk]] - LIVE, 0)
    tile = jnp.zeros((TILE, got.shape[2]), F32)
    for k in range(N_CHOL):
        tile += got[k, LIVE * ROWS_DEV :].astype(F32)
    row_id = lax.broadcasted_iota(jnp.int32, tile.shape, 0)
    for slot in range(LIVE):
        mine = slot < own
        live = mine | (slot - own < arriving)
        spot = jnp.where(mine, slot, jnp.clip(LIVE - 1 - slot + own, 0, LIVE - 1))
        first = spot * ORBS + jnp.maximum(spot - 2, 0) * TILE
        total = block[pl.ds(pl.multiple_of(first, TILE), ROWS_DEV)].astype(F32)
        rows = pl.ds(pl.multiple_of(spot * ROWS_DEV, ROWS_DEV), ROWS_DEV)
        for k in range(N_CHOL):
            total += got[k, rows].astype(F32)
        out[slot] = jnp.where(live, total, 0.0).astype(BF16)
        log_out[slot] = jnp.where(live, jnp.sum(jnp.where(row_id == spot, tile, 0.0)), 0.0)


def finish_call(counts, partner, got, block):
    lanes = got.shape[2]
    return pl.pallas_call(
        finish_kernel,
        in_specs=[SCALARS, SCALARS, WHOLE, WHOLE],
        out_specs=(WHOLE, SCALARS),
        out_shape=(
            jax.ShapeDtypeStruct((LIVE, ROWS_DEV, lanes), BF16),
            jax.ShapeDtypeStruct((LIVE,), F32),
        ),
        name="finish",
    )(counts, partner, got, block)


def shards(walkers, inv_intersection, fields, cholesky, trial_rows, counts, partner):
    walk_size = lax.axis_size("walk")
    outgoing = pack_call(walkers, inv_intersection, fields)
    received = []
    for bit in range(walk_size.bit_length() - 1):
        route = [(i, i ^ 1 << bit) for i in range(walk_size)]
        received.append(lax.ppermute(outgoing, "walk", route))
    block, x = merge_call(counts, partner, fields, walkers, inv_intersection, received)
    parts = ring(block)
    sums = product_call(x, cholesky, trial_rows, inv_intersection, parts)
    sums = lax.all_to_all(sums, "chol", 0, 0, tiled=True)
    return tuple(finish_call(counts, partner, sums, block))


def solution(mesh):
    in_specs = (
        P("walk", "chol", None),
        P("walk", None, None),
        P("walk", "chol"),
        P("chol", None, None),
        P(),
        P(),
        P(),
    )
    out_specs = (P("walk", "chol", None), P("walk"))
    return jax.shard_map(shards, mesh=mesh, in_specs=in_specs, out_specs=out_specs, check_vma=False)
```

```python
import jax
import jax.numpy as jnp
from jax import lax
from jax.experimental import pallas as pl
from jax.experimental.pallas import tpu as pltpu
from jax.sharding import PartitionSpec as P


ROWS_DEV = 64
LIVE = 4
MOVE = 2
STEP_ROOT = 0.1
N_CHOL = 8
OFFSETS = (0, -1, 1, -2, 2, -3, 3, -4)
TILE = 16
ORBS = 256
STRIDE = ORBS + TILE
RING_ROWS = 2 * STRIDE
FIELD_ROW = MOVE * STRIDE

ANY = pl.BlockSpec(memory_space=pl.ANY)
HBM = pl.BlockSpec(memory_space=pltpu.HBM)
WHOLE = pl.BlockSpec(memory_space=pltpu.VMEM)
SCALARS = pl.BlockSpec(memory_space=pltpu.SMEM)
F32 = jnp.float32
BF16 = jnp.bfloat16


def params(megabytes):
    return pltpu.CompilerParams(vmem_limit_bytes=megabytes << 20)


def after(value, *others):
    return lax.optimization_barrier((value, *others))[0]


def ring(block, gate=None):
    up = [(i, (i + 1) % N_CHOL) for i in range(N_CHOL)]
    down = [(i, (i - 1) % N_CHOL) for i in range(N_CHOL)]
    parts, low, high = [block], block, block
    for step in range(N_CHOL // 2):
        if step == 1 and gate is not None:
            low, high = after(low, gate), after(high, gate)
        low = lax.ppermute(low, "chol", up)
        parts.append(low)
        if step < N_CHOL // 2 - 1:
            high = lax.ppermute(high, "chol", down)
            parts.append(high)
    return parts


def inv_rows(inv, slot):
    share = pl.multiple_of(lax.axis_index("chol") * TILE, TILE)
    return inv.at[slot, pl.ds(share, TILE)]


def pack_kernel(counts, partner, walkers, inv, fields, out, early, kept, plan, sems):
    copies = []

    def add(source, target, first, size):
        copies.append(
            pltpu.make_async_copy(source, target.at[pl.ds(first, size)], sems.at[len(copies)])
        )

    for j in range(MOVE):
        add(walkers.at[LIVE + j], out, j * STRIDE, ORBS)
        add(inv_rows(inv, LIVE + j), out, j * STRIDE + ORBS, TILE)
    for j in range(MOVE):
        add(walkers.at[j], early, j * ORBS, ORBS)
        add(walkers.at[2 + j], kept, j * STRIDE, ORBS)
        add(inv_rows(inv, 2 + j), kept, j * STRIDE + ORBS, TILE)
    for copy in copies:
        copy.start()
    out[FIELD_ROW:] = jnp.zeros((TILE, out.shape[1]), BF16)
    out[FIELD_ROW : FIELD_ROW + fields.shape[0], : fields.shape[1]] = fields[...]
    walk = lax.axis_index("walk")
    mate = partner[walk]
    row_id = lax.broadcasted_iota(jnp.int32, plan.shape, 0)
    arriving = jnp.maximum(counts[mate] - LIVE, 0)
    rest = jnp.where(row_id == 1, counts[walk], arriving)
    plan[...] = jnp.where(row_id == 0, jnp.bitwise_xor(mate, walk), rest)
    for copy in copies:
        copy.wait()


def pack_call(counts, partner, walkers, inv, fields):
    lanes = walkers.shape[2]
    return pl.pallas_call(
        pack_kernel,
        in_specs=[SCALARS, SCALARS, HBM, HBM, WHOLE],
        out_specs=(WHOLE,) * 4,
        out_shape=(
            jax.ShapeDtypeStruct((FIELD_ROW + TILE, lanes), BF16),
            jax.ShapeDtypeStruct((2 * ORBS, lanes), BF16),
            jax.ShapeDtypeStruct((RING_ROWS, lanes), BF16),
            jax.ShapeDtypeStruct((8, lanes), jnp.int32),
        ),
        scratch_shapes=[pltpu.SemaphoreType.DMA((5 * MOVE,))],
        name="pack",
    )(counts, partner, walkers, inv, fields)


def merge_kernel(bits, plan, outgoing, kept, *refs):
    received, (out, x) = refs[:bits], refs[bits:]
    distance, own = plan[0:1], plan[1:2]

    def sent(rows, width):
        block = jnp.zeros((rows.stop - rows.start, width), F32)
        for bit in range(bits):
            here = distance[:, :width] == 1 << bit
            block = jnp.where(here, received[bit][rows, :width].astype(F32), block)
        return block

    lanes = out.shape[1]
    for q in range(2):
        for first in range(0, STRIDE, TILE):
            mine = kept[q * STRIDE + first : q * STRIDE + first + TILE].astype(F32)
            start = (1 - q) * STRIDE + first
            theirs = sent(slice(start, start + TILE), lanes)
            rows = slice(q * STRIDE + first, q * STRIDE + first + TILE)
            out[rows] = jnp.where(own > 2 + q, mine, theirs).astype(BF16)
    rows = slice(FIELD_ROW, FIELD_ROW + TILE)
    mine, theirs = outgoing[rows].astype(F32), sent(rows, lanes)
    for q in range(2):
        mask = own[:, q : q + 1] > 2 + q
        column = jnp.where(mask, mine[:, 2 + q : 3 + q], theirs[:, LIVE + 1 - q : LIVE + 2 - q])
        x[:, q : q + 1] = column


def merge_call(plan, outgoing, kept, received):
    bits, lanes = len(received), kept.shape[1]

    def body(*refs):
        merge_kernel(bits, *refs)

    return pl.pallas_call(
        body,
        in_specs=[WHOLE] * (3 + bits),
        out_specs=(WHOLE, WHOLE),
        out_shape=(
            jax.ShapeDtypeStruct((RING_ROWS, lanes), BF16),
            jax.ShapeDtypeStruct((TILE, lanes), F32),
        ),
        compiler_params=params(4),
        name="merge",
    )(plan, outgoing, kept, *received)


def product_kernel(late, x, chol, trial, extra, *refs):
    parts, out, minv = refs[:N_CHOL], refs[N_CHOL], refs[N_CHOL + 1]
    lanes = out.shape[2]
    stride, base = (STRIDE, 2) if late else (ORBS, 0)
    me = lax.axis_index("chol")
    owners = [jnp.bitwise_and(me + offset, N_CHOL - 1) for offset in OFFSETS]
    columns = [pl.ds(pl.multiple_of(owner * ORBS, ORBS), ORBS) for owner in owners]
    row_id = lax.broadcasted_iota(jnp.int32, (TILE, lanes), 0)
    lane_id = lax.broadcasted_iota(jnp.int32, (TILE, lanes), 1)
    logs = jnp.zeros((TILE, lanes), F32)
    if late:
        logs = extra[0, base * ROWS_DEV :].astype(F32)
        out[:, : base * ROWS_DEV] = extra[:, : base * ROWS_DEV]
        for owner, part in zip(owners, parts):
            share = pl.ds(pl.multiple_of(owner * TILE, TILE), TILE)
            for q in range(2):
                minv[q, share] = part[q * stride + ORBS : (q + 1) * stride]
    phi = jnp.concatenate(
        [
            jnp.concatenate([part[q * stride : q * stride + ORBS] for q in range(2)], axis=1)
            for part in parts
        ],
        axis=0,
    )
    products = []
    for g in range(chol.shape[0]):
        rows = jnp.concatenate([chol[g, :, spot] for spot in columns], axis=1)
        products.append(jnp.dot(rows, phi, preferred_element_type=F32))
    for q in range(2):
        weighted = lax.dot_general(
            trial[...],
            minv[q] if late else extra[q],
            (((1,), (1,)), ((), ())),
            preferred_element_type=F32,
        )
        total = jnp.zeros_like(weighted)
        log = jnp.zeros((1, 1), F32)
        for g, both in enumerate(products):
            product = both[:, q * lanes : (q + 1) * lanes]
            bias = -STEP_ROOT * jnp.sum(product * weighted, keepdims=True)
            field = x[g : g + 1, q : q + 1].astype(F32)
            total += STEP_ROOT * (field - bias) * product
            log += field * bias - 0.5 * bias * bias
        spread = total.astype(BF16).reshape(N_CHOL, ROWS_DEV, lanes)
        slot = base + q
        out[:, slot * ROWS_DEV : (slot + 1) * ROWS_DEV] = spread
        high = log.astype(BF16).astype(F32)
        here = row_id == slot
        logs = jnp.where(here & (lane_id == 0), high, logs)
        logs = jnp.where(here & (lane_id == 1), log - high, logs)
    for k in range(N_CHOL):
        out[k, (base + 2) * ROWS_DEV :] = logs.astype(BF16)


def product_call(late, x, cholesky, trial, extra, parts):
    lanes = trial.shape[1]
    vectors, window, orbitals = cholesky.shape
    flops = 4 * vectors * window * orbitals * lanes
    out_rows = (LIVE if late else 2) * ROWS_DEV + TILE

    def body(*refs):
        product_kernel(late, *refs)

    return pl.pallas_call(
        body,
        in_specs=[WHOLE] * (4 + N_CHOL),
        out_specs=WHOLE,
        out_shape=jax.ShapeDtypeStruct((N_CHOL, out_rows, lanes), BF16),
        scratch_shapes=[pltpu.VMEM((2, lanes, lanes), BF16)],
        compiler_params=params(24),
        name="late_products" if late else "early_products",
        cost_estimate=pl.CostEstimate(flops=flops, bytes_accessed=6 << 20, transcendentals=0),
    )(x, cholesky, trial, extra, *parts)


def finish_kernel(plan, got, early, late, out, log_out):
    own, arriving = plan[1:2], plan[2:3]
    tile = jnp.zeros((TILE, got.shape[2]), F32)
    for k in range(N_CHOL):
        tile += got[k, LIVE * ROWS_DEV :].astype(F32)
    walkers, logs = [], []
    for spot in range(LIVE):
        block, first = (early, spot * ORBS) if spot < 2 else (late, (spot - 2) * STRIDE)
        total = block[first : first + ROWS_DEV].astype(F32)
        for k in range(N_CHOL):
            total += got[k, spot * ROWS_DEV : (spot + 1) * ROWS_DEV].astype(F32)
        walkers.append(total)
        logs.append(tile[spot : spot + 1])
    for slot in range(LIVE):
        for values, store in ((walkers, True), (logs, False)):
            value = jnp.zeros_like(values[slot])
            for j in range(MOVE):
                moved = (own == slot - j) & (arriving > j)
                value = jnp.where(moved, values[LIVE - 1 - j], value)
            value = jnp.where(own > slot, values[slot], value)
            if store:
                out[slot] = value.astype(BF16)
            else:
                log_out[slot] = jnp.sum(value)


def finish_call(plan, got, early, late):
    lanes = got.shape[2]
    return pl.pallas_call(
        finish_kernel,
        in_specs=[WHOLE] * 4,
        out_specs=(WHOLE, SCALARS),
        out_shape=(
            jax.ShapeDtypeStruct((LIVE, ROWS_DEV, lanes), BF16),
            jax.ShapeDtypeStruct((LIVE,), F32),
        ),
        compiler_params=params(8),
        name="finish",
    )(plan, got, early, late)


def shards(walkers, inv_intersection, fields, cholesky, trial_rows, counts, partner):
    walk_size = lax.axis_size("walk")
    fields = fields.T
    outgoing, early, kept, plan = pack_call(
        counts, partner, walkers, inv_intersection, fields
    )
    received = []
    for bit in range(walk_size.bit_length() - 1):
        route = [(i, i ^ 1 << bit) for i in range(walk_size)]
        received.append(lax.ppermute(outgoing, "walk", route))
    early_parts = ring(early)
    late, x = merge_call(plan, outgoing, kept, received)
    first = product_call(
        False, fields, cholesky, trial_rows, inv_intersection, early_parts
    )
    late_parts = ring(late, first)
    sums = product_call(True, x, cholesky, trial_rows, first, late_parts)
    sums = lax.all_to_all(sums, "chol", 0, 0, tiled=True)
    return tuple(finish_call(plan, sums, early, late))


def solution(mesh):
    in_specs = (
        P("walk", "chol", None),
        P("walk", None, None),
        P("walk", "chol"),
        P("chol", None, None),
        P(),
        P(),
        P(),
    )
    out_specs = (P("walk", "chol", None), P("walk"))
    return jax.shard_map(shards, mesh=mesh, in_specs=in_specs, out_specs=out_specs, check_vma=False)
```

```python
import jax
import jax.numpy as jnp
from jax import lax
from jax.experimental import pallas as pl
from jax.experimental.pallas import tpu as pltpu
from jax.sharding import PartitionSpec as P


ROWS_DEV = 64
LIVE = 4
MOVE = 2
STEP_ROOT = 0.1
N_CHOL = 8
TILE = 16
ORBS = 256
STRIDE = ORBS + TILE
RING_ROWS = 2 * STRIDE
FIELD_ROW = MOVE * STRIDE

ANY = pl.BlockSpec(memory_space=pl.ANY)
HBM = pl.BlockSpec(memory_space=pltpu.HBM)
WHOLE = pl.BlockSpec(memory_space=pltpu.VMEM)
SCALARS = pl.BlockSpec(memory_space=pltpu.SMEM)
F32 = jnp.float32
BF16 = jnp.bfloat16


def params(megabytes):
    return pltpu.CompilerParams(vmem_limit_bytes=megabytes << 20)


def gather(copies):
    return lax.all_to_all(copies, "chol", 0, 0, tiled=True)


def inv_rows(inv, slot):
    share = pl.multiple_of(lax.axis_index("chol") * TILE, TILE)
    return inv.at[slot, pl.ds(share, TILE)]


def pack_kernel(counts, partner, walkers, inv, fields, out, early, kept, plan, sems):
    copies = []

    def add(source, target, first, size):
        copies.append(
            pltpu.make_async_copy(source, target.at[pl.ds(first, size)], sems.at[len(copies)])
        )

    for j in range(MOVE):
        add(walkers.at[LIVE + j], out, j * STRIDE, ORBS)
        add(inv_rows(inv, LIVE + j), out, j * STRIDE + ORBS, TILE)
    for j in range(MOVE):
        for k in range(N_CHOL):
            add(walkers.at[j], early.at[k], j * ORBS, ORBS)
        add(walkers.at[2 + j], kept, j * STRIDE, ORBS)
        add(inv_rows(inv, 2 + j), kept, j * STRIDE + ORBS, TILE)
    for copy in copies:
        copy.start()
    out[FIELD_ROW:] = jnp.zeros((TILE, out.shape[1]), BF16)
    out[FIELD_ROW : FIELD_ROW + fields.shape[0], : fields.shape[1]] = fields[...]
    walk = lax.axis_index("walk")
    mate = partner[walk]
    row_id = lax.broadcasted_iota(jnp.int32, plan.shape, 0)
    arriving = jnp.maximum(counts[mate] - LIVE, 0)
    rest = jnp.where(row_id == 1, counts[walk], arriving)
    plan[...] = jnp.where(row_id == 0, jnp.bitwise_xor(mate, walk), rest)
    for copy in copies:
        copy.wait()


def pack_call(counts, partner, walkers, inv, fields):
    lanes = walkers.shape[2]
    return pl.pallas_call(
        pack_kernel,
        in_specs=[SCALARS, SCALARS, HBM, HBM, WHOLE],
        out_specs=(WHOLE,) * 4,
        out_shape=(
            jax.ShapeDtypeStruct((FIELD_ROW + TILE, lanes), BF16),
            jax.ShapeDtypeStruct((N_CHOL, 2 * ORBS, lanes), BF16),
            jax.ShapeDtypeStruct((RING_ROWS, lanes), BF16),
            jax.ShapeDtypeStruct((8, lanes), jnp.int32),
        ),
        scratch_shapes=[pltpu.SemaphoreType.DMA(((4 + N_CHOL) * MOVE,))],
        name="pack",
    )(counts, partner, walkers, inv, fields)


def merge_kernel(bits, plan, outgoing, kept, *refs):
    received, (out, x) = refs[:bits], refs[bits:]
    distance, own = plan[0:1], plan[1:2]

    def sent(rows, width):
        block = jnp.zeros((rows.stop - rows.start, width), F32)
        for bit in range(bits):
            here = distance[:, :width] == 1 << bit
            block = jnp.where(here, received[bit][rows, :width].astype(F32), block)
        return block

    lanes = kept.shape[1]
    for q in range(2):
        for first in range(0, STRIDE, TILE):
            mine = kept[q * STRIDE + first : q * STRIDE + first + TILE].astype(F32)
            start = (1 - q) * STRIDE + first
            theirs = sent(slice(start, start + TILE), lanes)
            rows = slice(q * STRIDE + first, q * STRIDE + first + TILE)
            block = jnp.where(own > 2 + q, mine, theirs).astype(BF16)
            for k in range(N_CHOL):
                out[k, rows] = block
    rows = slice(FIELD_ROW, FIELD_ROW + TILE)
    mine, theirs = outgoing[rows].astype(F32), sent(rows, lanes)
    for q in range(2):
        mask = own[:, q : q + 1] > 2 + q
        column = jnp.where(mask, mine[:, 2 + q : 3 + q], theirs[:, LIVE + 1 - q : LIVE + 2 - q])
        x[:, q : q + 1] = column


def merge_call(plan, outgoing, kept, received):
    bits, lanes = len(received), kept.shape[1]

    def body(*refs):
        merge_kernel(bits, *refs)

    return pl.pallas_call(
        body,
        in_specs=[WHOLE] * (3 + bits),
        out_specs=(WHOLE, WHOLE),
        out_shape=(
            jax.ShapeDtypeStruct((N_CHOL, RING_ROWS, lanes), BF16),
            jax.ShapeDtypeStruct((TILE, lanes), F32),
        ),
        compiler_params=params(4),
        name="merge",
    )(plan, outgoing, kept, *received)


def product_kernel(late, x, chol, trial, extra, parts, out, minv):
    lanes = out.shape[2]
    stride, base = (STRIDE, 2) if late else (ORBS, 0)
    row_id = lax.broadcasted_iota(jnp.int32, (TILE, lanes), 0)
    lane_id = lax.broadcasted_iota(jnp.int32, (TILE, lanes), 1)
    logs = jnp.zeros((TILE, lanes), F32)
    if late:
        logs = extra[0, base * ROWS_DEV :].astype(F32)
        out[:, : base * ROWS_DEV] = extra[:, : base * ROWS_DEV]
        for k in range(N_CHOL):
            for q in range(2):
                rows = parts[k, q * stride + ORBS : (q + 1) * stride]
                minv[q, k * TILE : (k + 1) * TILE] = rows
    phi = jnp.concatenate(
        [
            jnp.concatenate([parts[k, q * stride : q * stride + ORBS] for q in range(2)], axis=1)
            for k in range(N_CHOL)
        ],
        axis=0,
    )
    products = []
    for g in range(chol.shape[0]):
        products.append(jnp.dot(chol[g], phi, preferred_element_type=F32))
    for q in range(2):
        weighted = lax.dot_general(
            trial[...],
            minv[q] if late else extra[q],
            (((1,), (1,)), ((), ())),
            preferred_element_type=F32,
        )
        total = jnp.zeros_like(weighted)
        log = jnp.zeros((1, 1), F32)
        for g, both in enumerate(products):
            product = both[:, q * lanes : (q + 1) * lanes]
            bias = -STEP_ROOT * jnp.sum(product * weighted, keepdims=True)
            field = x[g : g + 1, q : q + 1].astype(F32)
            total += STEP_ROOT * (field - bias) * product
            log += field * bias - 0.5 * bias * bias
        spread = total.astype(BF16).reshape(N_CHOL, ROWS_DEV, lanes)
        slot = base + q
        out[:, slot * ROWS_DEV : (slot + 1) * ROWS_DEV] = spread
        high = log.astype(BF16).astype(F32)
        here = row_id == slot
        logs = jnp.where(here & (lane_id == 0), high, logs)
        logs = jnp.where(here & (lane_id == 1), log - high, logs)
    for k in range(N_CHOL):
        out[k, (base + 2) * ROWS_DEV :] = logs.astype(BF16)


def product_call(late, x, cholesky, trial, extra, parts):
    lanes = trial.shape[1]
    vectors, window, orbitals = cholesky.shape
    flops = 4 * vectors * window * orbitals * lanes
    out_rows = (LIVE if late else 2) * ROWS_DEV + TILE

    def body(*refs):
        product_kernel(late, *refs)

    return pl.pallas_call(
        body,
        in_specs=[WHOLE] * 5,
        out_specs=WHOLE,
        out_shape=jax.ShapeDtypeStruct((N_CHOL, out_rows, lanes), BF16),
        scratch_shapes=[pltpu.VMEM((2, lanes, lanes), BF16)],
        compiler_params=params(24),
        name="late_products" if late else "early_products",
        cost_estimate=pl.CostEstimate(flops=flops, bytes_accessed=6 << 20, transcendentals=0),
    )(x, cholesky, trial, extra, parts)


def finish_kernel(plan, got, early, late, out, log_out):
    own, arriving = plan[1:2], plan[2:3]
    tile = jnp.zeros((TILE, got.shape[2]), F32)
    for k in range(N_CHOL):
        tile += got[k, LIVE * ROWS_DEV :].astype(F32)
    walkers, logs = [], []
    for spot in range(LIVE):
        block, first = (early, spot * ORBS) if spot < 2 else (late, (spot - 2) * STRIDE)
        total = block[0, first : first + ROWS_DEV].astype(F32)
        for k in range(N_CHOL):
            total += got[k, spot * ROWS_DEV : (spot + 1) * ROWS_DEV].astype(F32)
        walkers.append(total)
        logs.append(tile[spot : spot + 1])
    for slot in range(LIVE):
        for values, store in ((walkers, True), (logs, False)):
            value = jnp.zeros_like(values[slot])
            for j in range(MOVE):
                moved = (own == slot - j) & (arriving > j)
                value = jnp.where(moved, values[LIVE - 1 - j], value)
            value = jnp.where(own > slot, values[slot], value)
            if store:
                out[slot] = value.astype(BF16)
            else:
                log_out[slot] = jnp.sum(value)


def finish_call(plan, got, early, late):
    lanes = got.shape[2]
    return pl.pallas_call(
        finish_kernel,
        in_specs=[WHOLE] * 4,
        out_specs=(WHOLE, SCALARS),
        out_shape=(
            jax.ShapeDtypeStruct((LIVE, ROWS_DEV, lanes), BF16),
            jax.ShapeDtypeStruct((LIVE,), F32),
        ),
        compiler_params=params(8),
        name="finish",
    )(plan, got, early, late)


def shards(walkers, inv_intersection, fields, cholesky, trial_rows, counts, partner):
    walk_size = lax.axis_size("walk")
    fields = fields.T
    outgoing, early, kept, plan = pack_call(
        counts, partner, walkers, inv_intersection, fields
    )
    early_parts = gather(early)
    received = []
    for bit in range(walk_size.bit_length() - 1):
        route = [(i, i ^ 1 << bit) for i in range(walk_size)]
        received.append(lax.ppermute(outgoing, "walk", route))
    late, x = merge_call(plan, outgoing, kept, received)
    late_parts = gather(late)
    first = product_call(
        False, fields, cholesky, trial_rows, inv_intersection, early_parts
    )
    sums = product_call(True, x, cholesky, trial_rows, first, late_parts)
    sums = lax.all_to_all(sums, "chol", 0, 0, tiled=True)
    return tuple(finish_call(plan, sums, early, late))


def solution(mesh):
    in_specs = (
        P("walk", "chol", None),
        P("walk", None, None),
        P("walk", "chol"),
        P("chol", None, None),
        P(),
        P(),
        P(),
    )
    out_specs = (P("walk", "chol", None), P("walk"))
    return jax.shard_map(shards, mesh=mesh, in_specs=in_specs, out_specs=out_specs, check_vma=False)
```

```python
import jax
import jax.numpy as jnp
from jax import lax
from jax.experimental import pallas as pl
from jax.experimental.pallas import tpu as pltpu
from jax.sharding import PartitionSpec as P


ROWS_DEV = 64
LIVE = 4
MOVE = 2
STEP_ROOT = 0.1
N_CHOL = 8
OFFSETS = (0, -1, 1, -2, 2, -3, 3, -4)
TILE = 16
ORBS = 256
STRIDE = ORBS + TILE
RING_ROWS = 2 * STRIDE
FIELD_ROW = MOVE * STRIDE
DISTANCE, OWN, ARRIVING = 8, 9, 10

ANY = pl.BlockSpec(memory_space=pl.ANY)
HBM = pl.BlockSpec(memory_space=pltpu.HBM)
WHOLE = pl.BlockSpec(memory_space=pltpu.VMEM)
SCALARS = pl.BlockSpec(memory_space=pltpu.SMEM)
F32 = jnp.float32
BF16 = jnp.bfloat16


def params(megabytes):
    return pltpu.CompilerParams(vmem_limit_bytes=megabytes << 20)


def gather(copies):
    return lax.all_to_all(copies, "chol", 0, 0, tiled=True)


def gather_in_two(block):
    def shift(value, distance):
        route = [(i, (i + distance) % N_CHOL) for i in range(N_CHOL)]
        return lax.ppermute(value, "chol", route)

    low = shift(block, 2)
    high = shift(block, -2)
    below = shift(block, 1)
    above = shift(block, -1)
    far = shift(low, 2)
    return [block, below, above, low, high, shift(low, 1), shift(high, -1), far]


def inv_rows(inv, slot):
    share = pl.multiple_of(lax.axis_index("chol") * TILE, TILE)
    return inv.at[slot, pl.ds(share, TILE)]


def pack_kernel(counts, partner, walkers, inv, fields, out, early, kept, sems):
    copies = []

    def add(source, target, first, size):
        copies.append(
            pltpu.make_async_copy(source, target.at[pl.ds(first, size)], sems.at[len(copies)])
        )

    for j in range(MOVE):
        add(walkers.at[LIVE + j], out, j * STRIDE, ORBS)
        add(inv_rows(inv, LIVE + j), out, j * STRIDE + ORBS, TILE)
    for j in range(MOVE):
        for k in range(N_CHOL):
            add(walkers.at[j], early.at[k], j * ORBS, ORBS)
        add(walkers.at[2 + j], kept, j * STRIDE, ORBS)
        add(inv_rows(inv, 2 + j), kept, j * STRIDE + ORBS, TILE)
    for copy in copies:
        copy.start()
    out[FIELD_ROW:] = jnp.zeros((TILE, out.shape[1]), BF16)
    out[FIELD_ROW : FIELD_ROW + fields.shape[0], : fields.shape[1]] = fields[...]
    walk = lax.axis_index("walk")
    mate = partner[walk]
    row_id = lax.broadcasted_iota(jnp.int32, (TILE, kept.shape[1]), 0)
    plan = (jnp.bitwise_xor(mate, walk), counts[walk], jnp.maximum(counts[mate] - LIVE, 0))
    tile = jnp.zeros(row_id.shape, jnp.int32)
    for row, value in zip((DISTANCE, OWN, ARRIVING), plan):
        tile = jnp.where(row_id == row, value, tile)
    kept[FIELD_ROW:] = tile.astype(F32).astype(BF16)
    kept[FIELD_ROW : FIELD_ROW + fields.shape[0], : fields.shape[1]] = fields[...]
    for copy in copies:
        copy.wait()


def pack_call(counts, partner, walkers, inv, fields):
    lanes = walkers.shape[2]
    return pl.pallas_call(
        pack_kernel,
        in_specs=[SCALARS, SCALARS, HBM, HBM, WHOLE],
        out_specs=(WHOLE,) * 3,
        out_shape=(
            jax.ShapeDtypeStruct((FIELD_ROW + TILE, lanes), BF16),
            jax.ShapeDtypeStruct((N_CHOL, 2 * ORBS, lanes), BF16),
            jax.ShapeDtypeStruct((FIELD_ROW + TILE, lanes), BF16),
        ),
        scratch_shapes=[pltpu.SemaphoreType.DMA(((4 + N_CHOL) * MOVE,))],
        name="pack",
    )(counts, partner, walkers, inv, fields)


def merge_kernel(bits, kept, *refs):
    received, (out, x) = refs[:bits], refs[bits:]
    tile = kept[FIELD_ROW:].astype(F32)
    distance, own = tile[DISTANCE : DISTANCE + 1], tile[OWN : OWN + 1]

    def sent(rows, width):
        block = jnp.zeros((rows.stop - rows.start, width), F32)
        for bit in range(bits):
            here = distance[:, :width] == 1 << bit
            block = jnp.where(here, received[bit][rows, :width].astype(F32), block)
        return block

    lanes = kept.shape[1]
    row_id = lax.broadcasted_iota(jnp.int32, (TILE, 1), 0)
    for q in range(2):
        for first in range(0, STRIDE, TILE):
            mine = kept[q * STRIDE + first : q * STRIDE + first + TILE].astype(F32)
            start = (1 - q) * STRIDE + first
            theirs = sent(slice(start, start + TILE), lanes)
            rows = slice(q * STRIDE + first, q * STRIDE + first + TILE)
            block = jnp.where(own > 2 + q, mine, theirs).astype(BF16)
            out[rows] = block
    theirs = sent(slice(FIELD_ROW, FIELD_ROW + TILE), lanes)
    x[...] = tile
    for q in range(2):
        mask = (own[:, q : q + 1] > 2 + q) | (row_id >= DISTANCE)
        column = jnp.where(mask, tile[:, 2 + q : 3 + q], theirs[:, LIVE + 1 - q : LIVE + 2 - q])
        x[:, q : q + 1] = column


def merge_call(kept, received):
    bits, lanes = len(received), kept.shape[1]

    def body(*refs):
        merge_kernel(bits, *refs)

    return pl.pallas_call(
        body,
        in_specs=[WHOLE] * (1 + bits),
        out_specs=(WHOLE, WHOLE),
        out_shape=(
            jax.ShapeDtypeStruct((RING_ROWS, lanes), BF16),
            jax.ShapeDtypeStruct((TILE, lanes), F32),
        ),
        compiler_params=params(4),
        name="merge",
    )(kept, *received)


def product_kernel(late, x, chol, trial, extra, *refs):
    parts, (out, minv) = refs[:-2], refs[-2:]
    lanes = out.shape[2]
    stride, base = (STRIDE, 2) if late else (ORBS, 0)
    if late:
        me = lax.axis_index("chol")
        owners = [jnp.bitwise_and(me + offset, N_CHOL - 1) for offset in OFFSETS]
        columns = [pl.ds(pl.multiple_of(owner * ORBS, ORBS), ORBS) for owner in owners]
    else:
        parts = [parts[0].at[k] for k in range(N_CHOL)]
    row_id = lax.broadcasted_iota(jnp.int32, (TILE, lanes), 0)
    lane_id = lax.broadcasted_iota(jnp.int32, (TILE, lanes), 1)
    logs = jnp.zeros((TILE, lanes), F32)
    if late:
        logs = extra[0, base * ROWS_DEV :].astype(F32)
        out[:, : base * ROWS_DEV] = extra[:, : base * ROWS_DEV]
        for owner, part in zip(owners, parts):
            share = pl.ds(pl.multiple_of(owner * TILE, TILE), TILE)
            for q in range(2):
                minv[q, share] = part[q * stride + ORBS : (q + 1) * stride]
    phi = jnp.concatenate(
        [
            jnp.concatenate([part[q * stride : q * stride + ORBS] for q in range(2)], axis=1)
            for part in parts
        ],
        axis=0,
    )
    products = []
    for g in range(chol.shape[0]):
        rows = chol[g]
        if late:
            rows = jnp.concatenate([chol[g, :, spot] for spot in columns], axis=1)
        products.append(jnp.dot(rows, phi, preferred_element_type=F32))
    for q in range(2):
        weighted = lax.dot_general(
            trial[...],
            minv[q] if late else extra[q],
            (((1,), (1,)), ((), ())),
            preferred_element_type=F32,
        )
        total = jnp.zeros_like(weighted)
        log = jnp.zeros((1, 1), F32)
        for g, both in enumerate(products):
            product = both[:, q * lanes : (q + 1) * lanes]
            bias = -STEP_ROOT * jnp.sum(product * weighted, keepdims=True)
            field = x[g : g + 1, q : q + 1].astype(F32)
            total += STEP_ROOT * (field - bias) * product
            log += field * bias - 0.5 * bias * bias
        spread = total.astype(BF16).reshape(N_CHOL, ROWS_DEV, lanes)
        slot = base + q
        out[:, slot * ROWS_DEV : (slot + 1) * ROWS_DEV] = spread
        high = log.astype(BF16).astype(F32)
        here = row_id == slot
        logs = jnp.where(here & (lane_id == 0), high, logs)
        logs = jnp.where(here & (lane_id == 1), log - high, logs)
    for k in range(N_CHOL):
        out[k, (base + 2) * ROWS_DEV :] = logs.astype(BF16)


def product_call(late, x, cholesky, trial, extra, parts):
    lanes = trial.shape[1]
    vectors, window, orbitals = cholesky.shape
    flops = 4 * vectors * window * orbitals * lanes
    out_rows = (LIVE if late else 2) * ROWS_DEV + TILE

    def body(*refs):
        product_kernel(late, *refs)

    return pl.pallas_call(
        body,
        in_specs=[WHOLE] * (4 + len(parts)),
        out_specs=WHOLE,
        out_shape=jax.ShapeDtypeStruct((N_CHOL, out_rows, lanes), BF16),
        scratch_shapes=[pltpu.VMEM((2, lanes, lanes), BF16)],
        compiler_params=params(24),
        name="late_products" if late else "early_products",
        cost_estimate=pl.CostEstimate(flops=flops, bytes_accessed=6 << 20, transcendentals=0),
    )(x, cholesky, trial, extra, *parts)


def finish_kernel(x, got, early, late, out, log_out):
    own, arriving = x[OWN : OWN + 1], x[ARRIVING : ARRIVING + 1]
    tile = jnp.zeros((TILE, got.shape[2]), F32)
    for k in range(N_CHOL):
        tile += got[k, LIVE * ROWS_DEV :].astype(F32)
    walkers, logs = [], []
    for spot in range(LIVE):
        if spot < 2:
            total = early[0, spot * ORBS : spot * ORBS + ROWS_DEV].astype(F32)
        else:
            total = late[(spot - 2) * STRIDE : (spot - 2) * STRIDE + ROWS_DEV].astype(F32)
        for k in range(N_CHOL):
            total += got[k, spot * ROWS_DEV : (spot + 1) * ROWS_DEV].astype(F32)
        walkers.append(total)
        logs.append(tile[spot : spot + 1])
    for slot in range(LIVE):
        for values, store in ((walkers, True), (logs, False)):
            value = jnp.zeros_like(values[slot])
            for j in range(MOVE):
                moved = (own == slot - j) & (arriving > j)
                value = jnp.where(moved, values[LIVE - 1 - j], value)
            value = jnp.where(own > slot, values[slot], value)
            if store:
                out[slot] = value.astype(BF16)
            else:
                log_out[slot] = jnp.sum(value)


def finish_call(x, got, early, late):
    lanes = got.shape[2]
    return pl.pallas_call(
        finish_kernel,
        in_specs=[WHOLE] * 4,
        out_specs=(WHOLE, SCALARS),
        out_shape=(
            jax.ShapeDtypeStruct((LIVE, ROWS_DEV, lanes), BF16),
            jax.ShapeDtypeStruct((LIVE,), F32),
        ),
        compiler_params=params(8),
        name="finish",
    )(x, got, early, late)


def shards(walkers, inv_intersection, fields, cholesky, trial_rows, counts, partner):
    walk_size = lax.axis_size("walk")
    fields = fields.T
    outgoing, early, kept = pack_call(
        counts, partner, walkers, inv_intersection, fields
    )
    early_parts = gather(early)
    received = []
    for bit in range(walk_size.bit_length() - 1):
        route = [(i, i ^ 1 << bit) for i in range(walk_size)]
        received.append(lax.ppermute(outgoing, "walk", route))
    late, x = merge_call(kept, received)
    late_parts = gather_in_two(late)
    first = product_call(
        False, fields, cholesky, trial_rows, inv_intersection, [early_parts]
    )
    sums = product_call(True, x, cholesky, trial_rows, first, late_parts)
    sums = lax.all_to_all(sums, "chol", 0, 0, tiled=True)
    return tuple(finish_call(x, sums, early[:1], late))


def solution(mesh):
    in_specs = (
        P("walk", "chol", None),
        P("walk", None, None),
        P("walk", "chol"),
        P("chol", None, None),
        P(),
        P(),
        P(),
    )
    out_specs = (P("walk", "chol", None), P("walk"))
    return jax.shard_map(shards, mesh=mesh, in_specs=in_specs, out_specs=out_specs, check_vma=False)
```

```python
import jax
import jax.numpy as jnp
from jax import lax
from jax.experimental import pallas as pl
from jax.experimental.pallas import tpu as pltpu
from jax.sharding import PartitionSpec as P


ROWS_DEV = 64
LIVE = 4
MOVE = 2
STEP_ROOT = 0.1
N_CHOL = 8
OFFSETS = (0, -1, 1, -2, 2, -3, 3, -4)
TILE = 16
ORBS = 256
STRIDE = ORBS + TILE
RING_ROWS = 2 * STRIDE
FIELD_ROW = MOVE * STRIDE
DISTANCE, OWN, ARRIVING = 8, 9, 10

ANY = pl.BlockSpec(memory_space=pl.ANY)
HBM = pl.BlockSpec(memory_space=pltpu.HBM)
WHOLE = pl.BlockSpec(memory_space=pltpu.VMEM)
SCALARS = pl.BlockSpec(memory_space=pltpu.SMEM)
F32 = jnp.float32
BF16 = jnp.bfloat16


def params(megabytes):
    return pltpu.CompilerParams(vmem_limit_bytes=megabytes << 20)


def gather(copies):
    return lax.all_to_all(copies, "chol", 0, 0, tiled=True)


def gather_in_two(block):
    def shift(value, distance):
        route = [(i, (i + distance) % N_CHOL) for i in range(N_CHOL)]
        return lax.ppermute(value, "chol", route)

    low = shift(block, 2)
    high = shift(block, -2)
    below = shift(block, 1)
    above = shift(block, -1)
    far = shift(low, 2)
    return [block, below, above, low, high, shift(low, 1), shift(high, -1), far]


def inv_rows(inv, slot):
    share = pl.multiple_of(lax.axis_index("chol") * TILE, TILE)
    return inv.at[slot, pl.ds(share, TILE)]


def pack_kernel(counts, partner, walkers, inv, fields, out, early, kept, sems):
    copies = []

    def add(source, target, first, size):
        copies.append(
            pltpu.make_async_copy(source, target.at[pl.ds(first, size)], sems.at[len(copies)])
        )

    for j in range(MOVE):
        add(walkers.at[LIVE + j], out, j * STRIDE, ORBS)
        add(inv_rows(inv, LIVE + j), out, j * STRIDE + ORBS, TILE)
    for j in range(MOVE):
        for k in range(N_CHOL):
            add(walkers.at[j], early.at[k], j * ORBS, ORBS)
        add(walkers.at[2 + j], kept, j * STRIDE, ORBS)
        add(inv_rows(inv, 2 + j), kept, j * STRIDE + ORBS, TILE)
    for copy in copies:
        copy.start()
    out[FIELD_ROW:] = jnp.zeros((TILE, out.shape[1]), BF16)
    out[FIELD_ROW : FIELD_ROW + fields.shape[0], : fields.shape[1]] = fields[...]
    walk = lax.axis_index("walk")
    mate = partner[walk]
    row_id = lax.broadcasted_iota(jnp.int32, (TILE, kept.shape[1]), 0)
    plan = (jnp.bitwise_xor(mate, walk), counts[walk], jnp.maximum(counts[mate] - LIVE, 0))
    tile = jnp.zeros(row_id.shape, jnp.int32)
    for row, value in zip((DISTANCE, OWN, ARRIVING), plan):
        tile = jnp.where(row_id == row, value, tile)
    kept[FIELD_ROW:] = tile.astype(F32).astype(BF16)
    kept[FIELD_ROW : FIELD_ROW + fields.shape[0], : fields.shape[1]] = fields[...]
    for copy in copies:
        copy.wait()


def pack_call(counts, partner, walkers, inv, fields):
    lanes = walkers.shape[2]
    return pl.pallas_call(
        pack_kernel,
        in_specs=[SCALARS, SCALARS, HBM, HBM, WHOLE],
        out_specs=(WHOLE,) * 3,
        out_shape=(
            jax.ShapeDtypeStruct((FIELD_ROW + TILE, lanes), BF16),
            jax.ShapeDtypeStruct((N_CHOL, 2 * ORBS, lanes), BF16),
            jax.ShapeDtypeStruct((FIELD_ROW + TILE, lanes), BF16),
        ),
        scratch_shapes=[pltpu.SemaphoreType.DMA(((4 + N_CHOL) * MOVE,))],
        name="pack",
    )(counts, partner, walkers, inv, fields)


def merge_kernel(bits, kept, *refs):
    received, (out, x) = refs[:bits], refs[bits:]
    tile = kept[FIELD_ROW:].astype(F32)
    distance, own = tile[DISTANCE : DISTANCE + 1], tile[OWN : OWN + 1]

    def sent(rows, width):
        block = jnp.zeros((rows.stop - rows.start, width), F32)
        for bit in range(bits):
            here = distance[:, :width] == 1 << bit
            block = jnp.where(here, received[bit][rows, :width].astype(F32), block)
        return block

    lanes = kept.shape[1]
    row_id = lax.broadcasted_iota(jnp.int32, (TILE, 1), 0)
    for q in range(2):
        for first in range(0, STRIDE, TILE):
            mine = kept[q * STRIDE + first : q * STRIDE + first + TILE].astype(F32)
            start = (1 - q) * STRIDE + first
            theirs = sent(slice(start, start + TILE), lanes)
            rows = slice(q * STRIDE + first, q * STRIDE + first + TILE)
            block = jnp.where(own > 2 + q, mine, theirs).astype(BF16)
            out[rows] = block
    theirs = sent(slice(FIELD_ROW, FIELD_ROW + TILE), lanes)
    x[...] = tile
    for q in range(2):
        mask = (own[:, q : q + 1] > 2 + q) | (row_id >= DISTANCE)
        column = jnp.where(mask, tile[:, 2 + q : 3 + q], theirs[:, LIVE + 1 - q : LIVE + 2 - q])
        x[:, 2 + q : 3 + q] = column


def merge_call(kept, received):
    bits, lanes = len(received), kept.shape[1]

    def body(*refs):
        merge_kernel(bits, *refs)

    return pl.pallas_call(
        body,
        in_specs=[WHOLE] * (1 + bits),
        out_specs=(WHOLE, WHOLE),
        out_shape=(
            jax.ShapeDtypeStruct((RING_ROWS, lanes), BF16),
            jax.ShapeDtypeStruct((TILE, lanes), F32),
        ),
        compiler_params=params(4),
        name="merge",
    )(kept, *received)


def product_kernel(x, chol, trial, inv, early, *refs):
    parts, (out, vectors, products, minv, sems) = refs[:N_CHOL], refs[N_CHOL:]
    lanes = out.shape[2]
    half = chol.shape[1] // 2
    copies = []
    for g in range(chol.shape[0]):
        for h in range(2):
            rows = pl.ds(h * half, half)
            copies.append(
                pltpu.make_async_copy(chol.at[g, rows], vectors.at[g, rows], sems.at[g, h])
            )
    for copy in copies:
        copy.start()
    me = lax.axis_index("chol")
    owners = [jnp.bitwise_and(me + offset, N_CHOL - 1) for offset in OFFSETS]
    columns = [pl.ds(pl.multiple_of(owner * ORBS, ORBS), ORBS) for owner in owners]
    for owner, part in zip(owners, parts):
        share = pl.ds(pl.multiple_of(owner * TILE, TILE), TILE)
        for q in range(2):
            minv[q, share] = part[q * STRIDE + ORBS : (q + 1) * STRIDE]

    def side_by_side(block, stride):
        return jnp.concatenate([block[q * stride : q * stride + ORBS] for q in range(2)], axis=1)

    first = jnp.concatenate([side_by_side(early.at[k], ORBS) for k in range(N_CHOL)], axis=0)
    second = jnp.concatenate([side_by_side(part, STRIDE) for part in parts], axis=0)
    for g in range(chol.shape[0]):
        for h in range(2):
            copies[2 * g + h].wait()
            rows = slice(h * half, (h + 1) * half)
            products[0, g, rows] = jnp.dot(vectors[g, rows], first, preferred_element_type=F32)
            turned = jnp.concatenate([vectors[g, rows, spot] for spot in columns], axis=1)
            products[1, g, rows] = jnp.dot(turned, second, preferred_element_type=F32)
    row_id = lax.broadcasted_iota(jnp.int32, (TILE, lanes), 0)
    lane_id = lax.broadcasted_iota(jnp.int32, (TILE, lanes), 1)
    logs = jnp.zeros((TILE, lanes), F32)
    for slot in range(LIVE):
        pair, q = divmod(slot, 2)
        weighted = lax.dot_general(
            trial[...],
            minv[q] if pair else inv[q],
            (((1,), (1,)), ((), ())),
            preferred_element_type=F32,
        )
        total = jnp.zeros_like(weighted)
        log = jnp.zeros((1, 1), F32)
        for g in range(chol.shape[0]):
            product = products[pair, g, :, q * lanes : (q + 1) * lanes]
            bias = -STEP_ROOT * jnp.sum(product * weighted, keepdims=True)
            field = x[g : g + 1, slot : slot + 1]
            total += STEP_ROOT * (field - bias) * product
            log += field * bias - 0.5 * bias * bias
        spread = total.astype(BF16).reshape(N_CHOL, ROWS_DEV, lanes)
        out[:, slot * ROWS_DEV : (slot + 1) * ROWS_DEV] = spread
        high = log.astype(BF16).astype(F32)
        here = row_id == slot
        logs = jnp.where(here & (lane_id == 0), high, logs)
        logs = jnp.where(here & (lane_id == 1), log - high, logs)
    for k in range(N_CHOL):
        out[k, LIVE * ROWS_DEV :] = logs.astype(BF16)


def product_call(x, cholesky, trial, inv, early, parts):
    lanes = trial.shape[1]
    vectors, window, orbitals = cholesky.shape
    flops = 2 * LIVE * vectors * window * orbitals * lanes
    return pl.pallas_call(
        product_kernel,
        in_specs=[WHOLE, HBM, WHOLE, WHOLE, WHOLE] + [WHOLE] * len(parts),
        out_specs=WHOLE,
        out_shape=jax.ShapeDtypeStruct((N_CHOL, LIVE * ROWS_DEV + TILE, lanes), BF16),
        scratch_shapes=[
            pltpu.VMEM(cholesky.shape, BF16),
            pltpu.VMEM((2, vectors, window, 2 * lanes), F32),
            pltpu.VMEM((2, lanes, lanes), BF16),
            pltpu.SemaphoreType.DMA((vectors, 2)),
        ],
        compiler_params=params(48),
        name="products",
        cost_estimate=pl.CostEstimate(flops=flops, bytes_accessed=6 << 20, transcendentals=0),
    )(x, cholesky, trial, inv, early, *parts)


def finish_kernel(x, got, early, late, out, log_out):
    own, arriving = x[OWN : OWN + 1], x[ARRIVING : ARRIVING + 1]
    tile = jnp.zeros((TILE, got.shape[2]), F32)
    for k in range(N_CHOL):
        tile += got[k, LIVE * ROWS_DEV :].astype(F32)
    walkers, logs = [], []
    for spot in range(LIVE):
        if spot < 2:
            total = early[0, spot * ORBS : spot * ORBS + ROWS_DEV].astype(F32)
        else:
            total = late[(spot - 2) * STRIDE : (spot - 2) * STRIDE + ROWS_DEV].astype(F32)
        for k in range(N_CHOL):
            total += got[k, spot * ROWS_DEV : (spot + 1) * ROWS_DEV].astype(F32)
        walkers.append(total)
        logs.append(tile[spot : spot + 1])
    for slot in range(LIVE):
        for values, store in ((walkers, True), (logs, False)):
            value = jnp.zeros_like(values[slot])
            for j in range(MOVE):
                moved = (own == slot - j) & (arriving > j)
                value = jnp.where(moved, values[LIVE - 1 - j], value)
            value = jnp.where(own > slot, values[slot], value)
            if store:
                out[slot] = value.astype(BF16)
            else:
                log_out[slot] = jnp.sum(value)


def finish_call(x, got, early, late):
    lanes = got.shape[2]
    return pl.pallas_call(
        finish_kernel,
        in_specs=[WHOLE] * 4,
        out_specs=(WHOLE, SCALARS),
        out_shape=(
            jax.ShapeDtypeStruct((LIVE, ROWS_DEV, lanes), BF16),
            jax.ShapeDtypeStruct((LIVE,), F32),
        ),
        compiler_params=params(8),
        name="finish",
    )(x, got, early, late)


def shards(walkers, inv_intersection, fields, cholesky, trial_rows, counts, partner):
    walk_size = lax.axis_size("walk")
    fields = fields.T
    outgoing, early, kept = pack_call(
        counts, partner, walkers, inv_intersection, fields
    )
    early_parts = gather(early)
    received = []
    for bit in range(walk_size.bit_length() - 1):
        route = [(i, i ^ 1 << bit) for i in range(walk_size)]
        received.append(lax.ppermute(outgoing, "walk", route))
    late, x = merge_call(kept, received)
    late_parts = gather_in_two(late)
    sums = product_call(
        x, cholesky, trial_rows, inv_intersection, early_parts, late_parts
    )
    sums = lax.all_to_all(sums, "chol", 0, 0, tiled=True)
    return tuple(finish_call(x, sums, early[:1], late))


def solution(mesh):
    in_specs = (
        P("walk", "chol", None),
        P("walk", None, None),
        P("walk", "chol"),
        P("chol", None, None),
        P(),
        P(),
        P(),
    )
    out_specs = (P("walk", "chol", None), P("walk"))
    return jax.shard_map(shards, mesh=mesh, in_specs=in_specs, out_specs=out_specs, check_vma=False)
```

```python
import jax
import jax.numpy as jnp
from jax import lax
from jax.experimental import pallas as pl
from jax.experimental.pallas import tpu as pltpu
from jax.sharding import PartitionSpec as P


ROWS_DEV = 64
LIVE = 4
MOVE = 2
STEP_ROOT = 0.1
N_CHOL = 8
OFFSETS = (0, -1, 1, -2, 2, -3, 3, -4)
TILE = 16
ORBS = 256
STRIDE = ORBS + TILE
RING_ROWS = 2 * STRIDE
FIELD_ROW = MOVE * STRIDE
DISTANCE, OWN, ARRIVING = 8, 9, 10

ANY = pl.BlockSpec(memory_space=pl.ANY)
HBM = pl.BlockSpec(memory_space=pltpu.HBM)
WHOLE = pl.BlockSpec(memory_space=pltpu.VMEM)
SCALARS = pl.BlockSpec(memory_space=pltpu.SMEM)
F32 = jnp.float32
BF16 = jnp.bfloat16


def params(megabytes):
    return pltpu.CompilerParams(vmem_limit_bytes=megabytes << 20)


def gather(copies):
    return lax.all_to_all(copies, "chol", 0, 0, tiled=True)


def gather_in_two(block):
    def shift(value, distance):
        route = [(i, (i + distance) % N_CHOL) for i in range(N_CHOL)]
        return lax.ppermute(value, "chol", route)

    low = shift(block, 2)
    high = shift(block, -2)
    below = shift(block, 1)
    above = shift(block, -1)
    far = shift(low, 2)
    return [block, below, above, low, high, shift(low, 1), shift(high, -1), far]


def inv_rows(inv, slot):
    share = pl.multiple_of(lax.axis_index("chol") * TILE, TILE)
    return inv.at[slot, pl.ds(share, TILE)]


def run_copies(copies, between):
    for copy in copies:
        copy.start()
    between()
    for copy in copies:
        copy.wait()


def pack_kernel(walkers, inv, fields, out, sems):
    copies = []
    for j in range(MOVE):
        rows = out.at[pl.ds(j * STRIDE, ORBS)]
        copies.append(pltpu.make_async_copy(walkers.at[LIVE + j], rows, sems.at[2 * j]))
        rows = out.at[pl.ds(j * STRIDE + ORBS, TILE)]
        copies.append(pltpu.make_async_copy(inv_rows(inv, LIVE + j), rows, sems.at[2 * j + 1]))

    def rest():
        out[FIELD_ROW:] = jnp.zeros((TILE, out.shape[1]), BF16)
        out[FIELD_ROW : FIELD_ROW + fields.shape[0], : fields.shape[1]] = fields[...]

    run_copies(copies, rest)


def pack_call(walkers, inv, fields):
    return pl.pallas_call(
        pack_kernel,
        in_specs=[HBM, HBM, WHOLE],
        out_specs=WHOLE,
        out_shape=jax.ShapeDtypeStruct((FIELD_ROW + TILE, walkers.shape[2]), BF16),
        scratch_shapes=[pltpu.SemaphoreType.DMA((2 * MOVE,))],
        name="pack",
    )(walkers, inv, fields)


def keep_kernel(counts, partner, walkers, inv, fields, early, kept, sems):
    copies = []

    def add(source, target, first, size):
        copies.append(
            pltpu.make_async_copy(source, target.at[pl.ds(first, size)], sems.at[len(copies)])
        )

    for j in range(MOVE):
        for k in range(N_CHOL):
            add(walkers.at[j], early.at[k], j * ORBS, ORBS)
        add(walkers.at[2 + j], kept, j * STRIDE, ORBS)
        add(inv_rows(inv, 2 + j), kept, j * STRIDE + ORBS, TILE)

    def rest():
        walk = lax.axis_index("walk")
        mate = partner[walk]
        row_id = lax.broadcasted_iota(jnp.int32, (TILE, kept.shape[1]), 0)
        plan = (jnp.bitwise_xor(mate, walk), counts[walk], jnp.maximum(counts[mate] - LIVE, 0))
        tile = jnp.zeros(row_id.shape, jnp.int32)
        for row, value in zip((DISTANCE, OWN, ARRIVING), plan):
            tile = jnp.where(row_id == row, value, tile)
        kept[FIELD_ROW:] = tile.astype(F32).astype(BF16)
        kept[FIELD_ROW : FIELD_ROW + fields.shape[0], : fields.shape[1]] = fields[...]

    run_copies(copies, rest)


def keep_call(counts, partner, walkers, inv, fields):
    lanes = walkers.shape[2]
    return pl.pallas_call(
        keep_kernel,
        in_specs=[SCALARS, SCALARS, HBM, HBM, WHOLE],
        out_specs=(WHOLE, WHOLE),
        out_shape=(
            jax.ShapeDtypeStruct((N_CHOL, 2 * ORBS, lanes), BF16),
            jax.ShapeDtypeStruct((FIELD_ROW + TILE, lanes), BF16),
        ),
        scratch_shapes=[pltpu.SemaphoreType.DMA(((2 + N_CHOL) * MOVE,))],
        name="keep",
    )(counts, partner, walkers, inv, fields)


def merge_kernel(bits, kept, *refs):
    received, (out, x) = refs[:bits], refs[bits:]
    tile = kept[FIELD_ROW:].astype(F32)
    distance, own = tile[DISTANCE : DISTANCE + 1], tile[OWN : OWN + 1]

    def sent(rows, width):
        block = jnp.zeros((rows.stop - rows.start, width), F32)
        for bit in range(bits):
            here = distance[:, :width] == 1 << bit
            block = jnp.where(here, received[bit][rows, :width].astype(F32), block)
        return block

    lanes = kept.shape[1]
    row_id = lax.broadcasted_iota(jnp.int32, (TILE, 1), 0)
    for q in range(2):
        for first in range(0, STRIDE, TILE):
            mine = kept[q * STRIDE + first : q * STRIDE + first + TILE].astype(F32)
            start = (1 - q) * STRIDE + first
            theirs = sent(slice(start, start + TILE), lanes)
            rows = slice(q * STRIDE + first, q * STRIDE + first + TILE)
            block = jnp.where(own > 2 + q, mine, theirs).astype(BF16)
            out[rows] = block
    theirs = sent(slice(FIELD_ROW, FIELD_ROW + TILE), lanes)
    x[...] = tile
    for q in range(2):
        mask = (own[:, q : q + 1] > 2 + q) | (row_id >= DISTANCE)
        column = jnp.where(mask, tile[:, 2 + q : 3 + q], theirs[:, LIVE + 1 - q : LIVE + 2 - q])
        x[:, 2 + q : 3 + q] = column


def merge_call(kept, received):
    bits, lanes = len(received), kept.shape[1]

    def body(*refs):
        merge_kernel(bits, *refs)

    return pl.pallas_call(
        body,
        in_specs=[WHOLE] * (1 + bits),
        out_specs=(WHOLE, WHOLE),
        out_shape=(
            jax.ShapeDtypeStruct((RING_ROWS, lanes), BF16),
            jax.ShapeDtypeStruct((TILE, lanes), F32),
        ),
        compiler_params=params(4),
        name="merge",
    )(kept, *received)


def product_kernel(late, x, chol, trial, extra, *refs):
    parts, (out, minv) = refs[:-2], refs[-2:]
    lanes = out.shape[2]
    stride, base = (STRIDE, 2) if late else (ORBS, 0)
    if late:
        me = lax.axis_index("chol")
        owners = [jnp.bitwise_and(me + offset, N_CHOL - 1) for offset in OFFSETS]
        columns = [pl.ds(pl.multiple_of(owner * ORBS, ORBS), ORBS) for owner in owners]
    else:
        parts = [parts[0].at[k] for k in range(N_CHOL)]
    row_id = lax.broadcasted_iota(jnp.int32, (TILE, lanes), 0)
    lane_id = lax.broadcasted_iota(jnp.int32, (TILE, lanes), 1)
    logs = jnp.zeros((TILE, lanes), F32)
    if late:
        logs = extra[0, base * ROWS_DEV :].astype(F32)
        out[:, : base * ROWS_DEV] = extra[:, : base * ROWS_DEV]
        for owner, part in zip(owners, parts):
            share = pl.ds(pl.multiple_of(owner * TILE, TILE), TILE)
            for q in range(2):
                minv[q, share] = part[q * stride + ORBS : (q + 1) * stride]
    phi = jnp.concatenate(
        [
            jnp.concatenate([part[q * stride : q * stride + ORBS] for q in range(2)], axis=1)
            for part in parts
        ],
        axis=0,
    )
    products = []
    for g in range(chol.shape[0]):
        rows = chol[g]
        if late:
            rows = jnp.concatenate([chol[g, :, spot] for spot in columns], axis=1)
        products.append(jnp.dot(rows, phi, preferred_element_type=F32))
    for q in range(2):
        weighted = lax.dot_general(
            trial[...],
            minv[q] if late else extra[q],
            (((1,), (1,)), ((), ())),
            preferred_element_type=F32,
        )
        total = jnp.zeros_like(weighted)
        log = jnp.zeros((1, 1), F32)
        for g, both in enumerate(products):
            product = both[:, q * lanes : (q + 1) * lanes]
            bias = -STEP_ROOT * jnp.sum(product * weighted, keepdims=True)
            field = x[g : g + 1, base + q : base + q + 1]
            total += STEP_ROOT * (field - bias) * product
            log += field * bias - 0.5 * bias * bias
        spread = total.astype(BF16).reshape(N_CHOL, ROWS_DEV, lanes)
        slot = base + q
        out[:, slot * ROWS_DEV : (slot + 1) * ROWS_DEV] = spread
        high = log.astype(BF16).astype(F32)
        here = row_id == slot
        logs = jnp.where(here & (lane_id == 0), high, logs)
        logs = jnp.where(here & (lane_id == 1), log - high, logs)
    for k in range(N_CHOL):
        out[k, (base + 2) * ROWS_DEV :] = logs.astype(BF16)


def product_call(late, x, cholesky, trial, extra, parts):
    lanes = trial.shape[1]
    vectors, window, orbitals = cholesky.shape
    flops = 4 * vectors * window * orbitals * lanes
    out_rows = (LIVE if late else 2) * ROWS_DEV + TILE

    def body(*refs):
        product_kernel(late, *refs)

    return pl.pallas_call(
        body,
        in_specs=[WHOLE] * (4 + len(parts)),
        out_specs=WHOLE,
        out_shape=jax.ShapeDtypeStruct((N_CHOL, out_rows, lanes), BF16),
        scratch_shapes=[pltpu.VMEM((2, lanes, lanes), BF16)],
        compiler_params=params(24),
        name="late_products" if late else "early_products",
        cost_estimate=pl.CostEstimate(flops=flops, bytes_accessed=6 << 20, transcendentals=0),
    )(x, cholesky, trial, extra, *parts)


def finish_kernel(x, got, early, late, out, log_out):
    own, arriving = x[OWN : OWN + 1], x[ARRIVING : ARRIVING + 1]
    tile = jnp.zeros((TILE, got.shape[2]), F32)
    for k in range(N_CHOL):
        tile += got[k, LIVE * ROWS_DEV :].astype(F32)
    walkers, logs = [], []
    for spot in range(LIVE):
        if spot < 2:
            total = early[0, spot * ORBS : spot * ORBS + ROWS_DEV].astype(F32)
        else:
            total = late[(spot - 2) * STRIDE : (spot - 2) * STRIDE + ROWS_DEV].astype(F32)
        for k in range(N_CHOL):
            total += got[k, spot * ROWS_DEV : (spot + 1) * ROWS_DEV].astype(F32)
        walkers.append(total)
        logs.append(tile[spot : spot + 1])
    for slot in range(LIVE):
        for values, store in ((walkers, True), (logs, False)):
            value = jnp.zeros_like(values[slot])
            for j in range(MOVE):
                moved = (own == slot - j) & (arriving > j)
                value = jnp.where(moved, values[LIVE - 1 - j], value)
            value = jnp.where(own > slot, values[slot], value)
            if store:
                out[slot] = value.astype(BF16)
            else:
                log_out[slot] = jnp.sum(value)


def finish_call(x, got, early, late):
    lanes = got.shape[2]
    return pl.pallas_call(
        finish_kernel,
        in_specs=[WHOLE] * 4,
        out_specs=(WHOLE, SCALARS),
        out_shape=(
            jax.ShapeDtypeStruct((LIVE, ROWS_DEV, lanes), BF16),
            jax.ShapeDtypeStruct((LIVE,), F32),
        ),
        compiler_params=params(8),
        name="finish",
    )(x, got, early, late)


def shards(walkers, inv_intersection, fields, cholesky, trial_rows, counts, partner):
    walk_size = lax.axis_size("walk")
    fields = fields.T
    outgoing = pack_call(walkers, inv_intersection, fields)
    early, kept = keep_call(counts, partner, walkers, inv_intersection, fields)
    early_parts = gather(early)
    received = []
    for bit in range(walk_size.bit_length() - 1):
        route = [(i, i ^ 1 << bit) for i in range(walk_size)]
        received.append(lax.ppermute(outgoing, "walk", route))
    late, x = merge_call(kept, received)
    late_parts = gather_in_two(late)
    first = product_call(
        False, x, cholesky, trial_rows, inv_intersection, [early_parts]
    )
    sums = product_call(True, x, cholesky, trial_rows, first, late_parts)
    sums = lax.all_to_all(sums, "chol", 0, 0, tiled=True)
    return tuple(finish_call(x, sums, early[:1], late))


def solution(mesh):
    in_specs = (
        P("walk", "chol", None),
        P("walk", None, None),
        P("walk", "chol"),
        P("chol", None, None),
        P(),
        P(),
        P(),
    )
    out_specs = (P("walk", "chol", None), P("walk"))
    return jax.shard_map(shards, mesh=mesh, in_specs=in_specs, out_specs=out_specs, check_vma=False)
```

```python
import jax
import jax.numpy as jnp
from jax import lax
from jax.experimental import pallas as pl
from jax.experimental.pallas import tpu as pltpu
from jax.sharding import PartitionSpec as P


ROWS_DEV = 64
LIVE = 4
MOVE = 2
STEP_ROOT = 0.1
N_CHOL = 8
OFFSETS = (0, -1, 1, -2, 2, -3, 3, -4)
TILE = 16
ORBS = 256
STRIDE = ORBS + TILE
RING_ROWS = 2 * STRIDE
FIELD_ROW = MOVE * STRIDE
DISTANCE, OWN, ARRIVING = 8, 9, 10

ANY = pl.BlockSpec(memory_space=pl.ANY)
HBM = pl.BlockSpec(memory_space=pltpu.HBM)
WHOLE = pl.BlockSpec(memory_space=pltpu.VMEM)
SCALARS = pl.BlockSpec(memory_space=pltpu.SMEM)
F32 = jnp.float32
BF16 = jnp.bfloat16


def params(megabytes):
    return pltpu.CompilerParams(vmem_limit_bytes=megabytes << 20)


def gather(copies):
    return lax.all_to_all(copies, "chol", 0, 0, tiled=True)


def gather_in_two(block):
    def shift(value, distance):
        route = [(i, (i + distance) % N_CHOL) for i in range(N_CHOL)]
        return lax.ppermute(value, "chol", route)

    low = shift(block, 2)
    high = shift(block, -2)
    below = shift(block, 1)
    above = shift(block, -1)
    far = shift(low, 2)
    return [block, below, above, low, high, shift(low, 1), shift(high, -1), far]


def inv_rows(inv, slot):
    share = pl.multiple_of(lax.axis_index("chol") * TILE, TILE)
    return inv.at[slot, pl.ds(share, TILE)]


def run_copies(copies, between):
    for copy in copies:
        copy.start()
    between()
    for copy in copies:
        copy.wait()


def pack_kernel(walkers, inv, fields, out, sems):
    copies = []
    for j in range(MOVE):
        rows = out.at[pl.ds(j * STRIDE, ORBS)]
        copies.append(pltpu.make_async_copy(walkers.at[LIVE + j], rows, sems.at[2 * j]))
        rows = out.at[pl.ds(j * STRIDE + ORBS, TILE)]
        copies.append(pltpu.make_async_copy(inv_rows(inv, LIVE + j), rows, sems.at[2 * j + 1]))

    def rest():
        out[FIELD_ROW:] = jnp.zeros((TILE, out.shape[1]), BF16)
        out[FIELD_ROW : FIELD_ROW + fields.shape[0], : fields.shape[1]] = fields[...]

    run_copies(copies, rest)


def pack_call(walkers, inv, fields):
    return pl.pallas_call(
        pack_kernel,
        in_specs=[HBM, HBM, WHOLE],
        out_specs=WHOLE,
        out_shape=jax.ShapeDtypeStruct((FIELD_ROW + TILE, walkers.shape[2]), BF16),
        scratch_shapes=[pltpu.SemaphoreType.DMA((2 * MOVE,))],
        name="pack",
    )(walkers, inv, fields)


def keep_kernel(counts, partner, walkers, inv, fields, early, kept, sems):
    copies = []

    def add(source, target, first, size):
        copies.append(
            pltpu.make_async_copy(source, target.at[pl.ds(first, size)], sems.at[len(copies)])
        )

    for j in range(MOVE):
        add(walkers.at[j], early.at[0], j * ORBS, ORBS)
        add(walkers.at[2 + j], kept, j * STRIDE, ORBS)
        add(inv_rows(inv, 2 + j), kept, j * STRIDE + ORBS, TILE)

    def rest():
        walk = lax.axis_index("walk")
        mate = partner[walk]
        row_id = lax.broadcasted_iota(jnp.int32, (TILE, kept.shape[1]), 0)
        plan = (jnp.bitwise_xor(mate, walk), counts[walk], jnp.maximum(counts[mate] - LIVE, 0))
        tile = jnp.zeros(row_id.shape, jnp.int32)
        for row, value in zip((DISTANCE, OWN, ARRIVING), plan):
            tile = jnp.where(row_id == row, value, tile)
        kept[FIELD_ROW:] = tile.astype(F32).astype(BF16)
        kept[FIELD_ROW : FIELD_ROW + fields.shape[0], : fields.shape[1]] = fields[...]

    run_copies(copies, rest)
    block = early[0]
    for k in range(1, N_CHOL):
        early[k] = block


def keep_call(counts, partner, walkers, inv, fields):
    lanes = walkers.shape[2]
    return pl.pallas_call(
        keep_kernel,
        in_specs=[SCALARS, SCALARS, HBM, HBM, WHOLE],
        out_specs=(WHOLE, WHOLE),
        out_shape=(
            jax.ShapeDtypeStruct((N_CHOL, 2 * ORBS, lanes), BF16),
            jax.ShapeDtypeStruct((FIELD_ROW + TILE, lanes), BF16),
        ),
        scratch_shapes=[pltpu.SemaphoreType.DMA((3 * MOVE,))],
        name="keep",
    )(counts, partner, walkers, inv, fields)


def merge_kernel(bits, kept, *refs):
    received, (out, x) = refs[:bits], refs[bits:]
    tile = kept[FIELD_ROW:].astype(F32)
    distance, own = tile[DISTANCE : DISTANCE + 1], tile[OWN : OWN + 1]

    def sent(rows, width):
        block = jnp.zeros((rows.stop - rows.start, width), F32)
        for bit in range(bits):
            here = distance[:, :width] == 1 << bit
            block = jnp.where(here, received[bit][rows, :width].astype(F32), block)
        return block

    lanes = kept.shape[1]
    row_id = lax.broadcasted_iota(jnp.int32, (TILE, 1), 0)
    for q in range(2):
        for first in range(0, STRIDE, TILE):
            mine = kept[q * STRIDE + first : q * STRIDE + first + TILE].astype(F32)
            start = (1 - q) * STRIDE + first
            theirs = sent(slice(start, start + TILE), lanes)
            rows = slice(q * STRIDE + first, q * STRIDE + first + TILE)
            block = jnp.where(own > 2 + q, mine, theirs).astype(BF16)
            out[rows] = block
    theirs = sent(slice(FIELD_ROW, FIELD_ROW + TILE), lanes)
    x[...] = tile
    for q in range(2):
        mask = (own[:, q : q + 1] > 2 + q) | (row_id >= DISTANCE)
        column = jnp.where(mask, tile[:, 2 + q : 3 + q], theirs[:, LIVE + 1 - q : LIVE + 2 - q])
        x[:, 2 + q : 3 + q] = column


def merge_call(kept, received):
    bits, lanes = len(received), kept.shape[1]

    def body(*refs):
        merge_kernel(bits, *refs)

    return pl.pallas_call(
        body,
        in_specs=[WHOLE] * (1 + bits),
        out_specs=(WHOLE, WHOLE),
        out_shape=(
            jax.ShapeDtypeStruct((RING_ROWS, lanes), BF16),
            jax.ShapeDtypeStruct((TILE, lanes), F32),
        ),
        compiler_params=params(4),
        name="merge",
    )(kept, *received)


def product_kernel(late, x, chol, trial, extra, *refs):
    parts, (out, minv) = refs[:-2], refs[-2:]
    lanes = out.shape[2]
    stride, base = (STRIDE, 2) if late else (ORBS, 0)
    if late:
        me = lax.axis_index("chol")
        owners = [jnp.bitwise_and(me + offset, N_CHOL - 1) for offset in OFFSETS]
        columns = [pl.ds(pl.multiple_of(owner * ORBS, ORBS), ORBS) for owner in owners]
    else:
        parts = [parts[0].at[k] for k in range(N_CHOL)]
    row_id = lax.broadcasted_iota(jnp.int32, (TILE, lanes), 0)
    lane_id = lax.broadcasted_iota(jnp.int32, (TILE, lanes), 1)
    logs = jnp.zeros((TILE, lanes), F32)
    if late:
        logs = extra[0, base * ROWS_DEV :].astype(F32)
        out[:, : base * ROWS_DEV] = extra[:, : base * ROWS_DEV]
        for owner, part in zip(owners, parts):
            share = pl.ds(pl.multiple_of(owner * TILE, TILE), TILE)
            for q in range(2):
                minv[q, share] = part[q * stride + ORBS : (q + 1) * stride]
    phi = jnp.concatenate(
        [
            jnp.concatenate([part[q * stride : q * stride + ORBS] for q in range(2)], axis=1)
            for part in parts
        ],
        axis=0,
    )
    products = []
    for g in range(chol.shape[0]):
        rows = chol[g]
        if late:
            rows = jnp.concatenate([chol[g, :, spot] for spot in columns], axis=1)
        products.append(jnp.dot(rows, phi, preferred_element_type=F32))
    for q in range(2):
        weighted = lax.dot_general(
            trial[...],
            minv[q] if late else extra[q],
            (((1,), (1,)), ((), ())),
            preferred_element_type=F32,
        )
        total = jnp.zeros_like(weighted)
        log = jnp.zeros((1, 1), F32)
        for g, both in enumerate(products):
            product = both[:, q * lanes : (q + 1) * lanes]
            bias = -STEP_ROOT * jnp.sum(product * weighted, keepdims=True)
            field = x[g : g + 1, base + q : base + q + 1]
            total += STEP_ROOT * (field - bias) * product
            log += field * bias - 0.5 * bias * bias
        spread = total.astype(BF16).reshape(N_CHOL, ROWS_DEV, lanes)
        slot = base + q
        out[:, slot * ROWS_DEV : (slot + 1) * ROWS_DEV] = spread
        high = log.astype(BF16).astype(F32)
        here = row_id == slot
        logs = jnp.where(here & (lane_id == 0), high, logs)
        logs = jnp.where(here & (lane_id == 1), log - high, logs)
    for k in range(N_CHOL):
        out[k, (base + 2) * ROWS_DEV :] = logs.astype(BF16)


def product_call(late, x, cholesky, trial, extra, parts):
    lanes = trial.shape[1]
    vectors, window, orbitals = cholesky.shape
    flops = 4 * vectors * window * orbitals * lanes
    out_rows = (LIVE if late else 2) * ROWS_DEV + TILE

    def body(*refs):
        product_kernel(late, *refs)

    return pl.pallas_call(
        body,
        in_specs=[WHOLE] * (4 + len(parts)),
        out_specs=WHOLE,
        out_shape=jax.ShapeDtypeStruct((N_CHOL, out_rows, lanes), BF16),
        scratch_shapes=[pltpu.VMEM((2, lanes, lanes), BF16)],
        compiler_params=params(24),
        name="late_products" if late else "early_products",
        cost_estimate=pl.CostEstimate(flops=flops, bytes_accessed=6 << 20, transcendentals=0),
    )(x, cholesky, trial, extra, *parts)


def finish_kernel(x, got, early, late, out, log_out):
    own, arriving = x[OWN : OWN + 1], x[ARRIVING : ARRIVING + 1]
    tile = jnp.zeros((TILE, got.shape[2]), F32)
    for k in range(N_CHOL):
        tile += got[k, LIVE * ROWS_DEV :].astype(F32)
    walkers, logs = [], []
    for spot in range(LIVE):
        if spot < 2:
            total = early[0, spot * ORBS : spot * ORBS + ROWS_DEV].astype(F32)
        else:
            total = late[(spot - 2) * STRIDE : (spot - 2) * STRIDE + ROWS_DEV].astype(F32)
        for k in range(N_CHOL):
            total += got[k, spot * ROWS_DEV : (spot + 1) * ROWS_DEV].astype(F32)
        walkers.append(total)
        logs.append(tile[spot : spot + 1])
    for slot in range(LIVE):
        for values, store in ((walkers, True), (logs, False)):
            value = jnp.zeros_like(values[slot])
            for j in range(MOVE):
                moved = (own == slot - j) & (arriving > j)
                value = jnp.where(moved, values[LIVE - 1 - j], value)
            value = jnp.where(own > slot, values[slot], value)
            if store:
                out[slot] = value.astype(BF16)
            else:
                log_out[slot] = jnp.sum(value)


def finish_call(x, got, early, late):
    lanes = got.shape[2]
    return pl.pallas_call(
        finish_kernel,
        in_specs=[WHOLE] * 4,
        out_specs=(WHOLE, SCALARS),
        out_shape=(
            jax.ShapeDtypeStruct((LIVE, ROWS_DEV, lanes), BF16),
            jax.ShapeDtypeStruct((LIVE,), F32),
        ),
        compiler_params=params(8),
        name="finish",
    )(x, got, early, late)


def shards(walkers, inv_intersection, fields, cholesky, trial_rows, counts, partner):
    walk_size = lax.axis_size("walk")
    fields = fields.T
    outgoing = pack_call(walkers, inv_intersection, fields)
    early, kept = keep_call(counts, partner, walkers, inv_intersection, fields)
    early_parts = gather(early)
    received = []
    for bit in range(walk_size.bit_length() - 1):
        route = [(i, i ^ 1 << bit) for i in range(walk_size)]
        received.append(lax.ppermute(outgoing, "walk", route))
    late, x = merge_call(kept, received)
    late_parts = gather_in_two(late)
    first = product_call(
        False, x, cholesky, trial_rows, inv_intersection, [early_parts]
    )
    sums = product_call(True, x, cholesky, trial_rows, first, late_parts)
    sums = lax.all_to_all(sums, "chol", 0, 0, tiled=True)
    return tuple(finish_call(x, sums, early[:1], late))


def solution(mesh):
    in_specs = (
        P("walk", "chol", None),
        P("walk", None, None),
        P("walk", "chol"),
        P("chol", None, None),
        P(),
        P(),
        P(),
    )
    out_specs = (P("walk", "chol", None), P("walk"))
    return jax.shard_map(shards, mesh=mesh, in_specs=in_specs, out_specs=out_specs, check_vma=False)
```
